32 devices in a mesh: ckpt: 8 (over y, x, core), vocab: 4 (over z).
Axes of the slice: x: 2, y: 2, z: 4, core: 2. Of those that a mesh axis runs over, the one named last changes fastest.
Arguments:
- hidden_rows: bfloat16 [8, 128, 768], P('ckpt'), may hold values from -8 to 8
- norm_gain: float32 [8, 768], P('ckpt'), may hold values from 0.5 to 1.5
- norm_bias: float32 [8, 768], P('ckpt'), may hold values from -1.2 to 1.2
- unembed: bfloat16 [8, 768, 50304], P('ckpt', None, 'vocab'), may hold values from -6 to 6
- target_ids: int32 [128], replicated, may hold values from 0 to 50303
- ckpt_steps: int32 [8], replicated, may hold values from 0 to 143000
- components: int32 [1], replicated, may hold values from 1 to 8
Outputs:
- loadings: bfloat16 [8, 128, 50304], P(None, 'ckpt', 'vocab')
- gram: float32 [8, 8], replicated
- target_logprob: float32 [8, 128], P('ckpt')
The draws below stay inside these ranges and needn't reach their ends.
All inputs are finite; a program needn't handle non-finite values.
Results may differ from the reference program's by a relative error of at most 0.0063.
Values may be sent and summed in bfloat16 or wider, within the bound.
A program may use at most 192 MiB of HBM per device.

```python
import jax
import jax.numpy as jnp
from jax import lax

D = 768
V = 50304
TOK_SLAB = 16
COMPONENTS = 8
CKPTS = 8
TOKENS = 128
N_CKPT = 8


def unit_draw(key, shape):
    return jax.random.normal(key, shape, jnp.float32)


def mixture():
    return (0.8, 0.45, 0.4)


def drift_weights(key, directions):
    increments = jax.random.normal(key, (CKPTS, directions), jnp.float32)
    walk = jnp.cumsum(increments, axis=0)
    walk = walk - jnp.mean(walk, axis=0, keepdims=True)
    spread = jnp.sqrt(jnp.mean(walk * walk, axis=0, keepdims=True))
    return walk / (spread + 0.001)


def column_boost(key):
    length = max(V // 192, 1)
    starts = jax.random.randint(jax.random.fold_in(key, 27), (8,), 0, V - length + 1)
    strength = jnp.exp(jax.random.uniform(jax.random.fold_in(key, 28), (8,), jnp.float32, 0.693, 1.609))
    positions = jnp.arange(V, dtype=jnp.int32)
    inside = (positions[None, :] >= starts[:, None]) & (positions[None, :] < starts[:, None] + length)
    return jnp.max(jnp.where(inside, strength[:, None], 1.0), axis=0)


def base_hidden(key):
    shared_part, drift_part, noise_part = mixture()
    shared = unit_draw(jax.random.fold_in(key, 11), (TOKENS, D))
    paths = unit_draw(jax.random.fold_in(key, 13), (4, TOKENS, D))
    weights = drift_weights(jax.random.fold_in(key, 14), 4)
    drift = jnp.einsum('cj,jtd->ctd', weights, paths) / 2.0
    noise = unit_draw(jax.random.fold_in(key, 15), (CKPTS, TOKENS, D))
    values = shared_part * shared[None, :, :] + drift_part * drift + noise_part * noise
    return jnp.clip(values, -8.0, 8.0)


def draw_hidden_rows(key, part):
    return base_hidden(key).astype(jnp.bfloat16)


def draw_unembed(key, part):
    scale = 3.0 / jnp.sqrt(jnp.float32(D))
    bound = 4.0 + 2000 // D
    shared_part, drift_part, noise_part = mixture()
    shared = unit_draw(jax.random.fold_in(key, 21), (D, V))
    paths = unit_draw(jax.random.fold_in(key, 24), (4, D, V))
    weights = drift_weights(jax.random.fold_in(key, 25), 4)
    boost = column_boost(key)
    noise_key = jax.random.fold_in(key, 26)

    def one_ckpt(index):
        noise = unit_draw(jax.random.fold_in(noise_key, index), (D, V))
        drift = jnp.tensordot(weights[index], paths, axes=1) / 2.0 * boost[None, :]
        matrix = (shared_part * shared + drift_part * drift + noise_part * noise) * scale
        return jnp.clip(matrix, -bound, bound).astype(jnp.bfloat16)
    return lax.map(one_ckpt, jnp.arange(CKPTS, dtype=jnp.int32))


def with_ends(drawn, stream_key, smallest, high):
    longest = drawn.shape.index(max(drawn.shape))
    spots = []
    for shift in (0, 1):
        where = [jax.random.randint(jax.random.fold_in(stream_key, axis), (), 0, length) for axis, length in enumerate(drawn.shape)]
        where[longest] = (where[longest] + shift) % drawn.shape[longest]
        spots.append(tuple(where))
    return drawn.at[spots[0]].set(smallest).at[spots[1]].set(high)


def shard_levels(own_key, extent, shards, low, top_value):
    def one(position, shards_of):
        draws = jax.random.uniform(jax.random.fold_in(jax.random.fold_in(own_key, 6), position), (shards_of,), jnp.float32, low / len(shards), top_value / len(shards))
        return jnp.repeat(jnp.exp(draws), extent[position] // shards_of).reshape((-1,) + (1,) * (len(extent) - position - 1))

    factor_of = one(*shards[0])
    for cut in shards[1:]:
        factor_of = factor_of * one(*cut)
    return factor_of


def bell_draw(own_key, dims, scale, reach, cuts=(), held_as=jnp.bfloat16):
    level = shard_levels(own_key, dims, cuts, -0.22, 0.18) if cuts else 1.0
    drawn = jax.random.normal(own_key, dims, jnp.float32) * scale * level
    return jnp.minimum(jnp.maximum(drawn, -reach), reach).astype(held_as)


def setup_inputs(seed: int = 0) -> dict:
    key_list = jax.random.split(jax.random.key(seed), 8)
    return {
        "hidden_rows": draw_hidden_rows(jax.random.fold_in(key_list[7], 71), 0),
        "norm_gain": jnp.clip(1.0 + 0.1 * jax.random.normal(key_list[1], (CKPTS, D), jnp.float32), 0.5, 1.5),
        "norm_bias": bell_draw(key_list[2], (CKPTS, D), 0.2, 1.2, ((0, 8),), jnp.float32),
        "unembed": draw_unembed(jax.random.fold_in(key_list[7], 71), 0),
        "target_ids": with_ends(jax.random.randint(key_list[4], (TOKENS,), 0, V), jax.random.fold_in(key_list[4], 1), 0, V - 1).astype(jnp.int32),
        "ckpt_steps": with_ends(jax.random.randint(key_list[5], (CKPTS,), 0, 143001), jax.random.fold_in(key_list[5], 1), 0, 143000).astype(jnp.int32),
        "components": jax.random.randint(key_list[6], (1,), 1, COMPONENTS + 1).astype(jnp.int32),
    }


def one_checkpoint(items, target_ids):
    rows, gain, bias, weights = items
    floats = rows.astype(jnp.float32)
    centre = lax.optimization_barrier(jnp.mean(floats, axis=1, keepdims=True))
    spread = lax.optimization_barrier(jnp.mean((floats - centre) ** 2, axis=1, keepdims=True))
    normed = ((floats - centre) / jnp.sqrt(spread + 1e-05) * gain[None, :] + bias[None, :]).astype(jnp.bfloat16)
    logits = jnp.dot(normed, weights, preferred_element_type=jnp.float32)
    top = lax.optimization_barrier(jnp.max(logits, axis=1, keepdims=True))
    lse = top + jnp.log(lax.optimization_barrier(jnp.sum(jnp.exp(logits - top), axis=1, keepdims=True)))
    logprob = (logits - lse).astype(jnp.bfloat16)
    picked = jnp.take_along_axis(logits, target_ids[:, None].astype(jnp.int32), axis=1)
    return (logprob, (picked - lse)[:, 0])

def slab_centred(logprob_all, index):
    piece = lax.dynamic_slice_in_dim(logprob_all, (index * TOK_SLAB).astype(jnp.int32), TOK_SLAB, 1)
    floats = piece.astype(jnp.float32)
    return floats - lax.optimization_barrier(jnp.mean(floats, axis=0, keepdims=True))

def reference(hidden_rows, norm_gain, norm_bias, unembed, target_ids, ckpt_steps, components):
    logprob_all, target_logprob = lax.map(lambda items: one_checkpoint(items, target_ids), (hidden_rows, norm_gain, norm_bias, unembed))
    slab_index = jnp.arange(N_CKPT, dtype=jnp.int32)

    def add_slab(total, index):
        centred = slab_centred(logprob_all, index)
        part = jnp.einsum('ctv,dtv->cd', centred, centred, precision=lax.Precision.HIGHEST)
        return (total + part, None)
    total, unused = lax.scan(add_slab, jnp.zeros((CKPTS, CKPTS), jnp.float32), slab_index)
    gram = total / (TOKENS * V)
    freqs = jnp.arange(COMPONENTS).astype(jnp.float32) + 1.0
    basis = jnp.cos(jnp.pi * freqs[None, :] * ckpt_steps.astype(jnp.float32)[:, None] / 143000.0)
    trace = jnp.sum(jnp.diagonal(gram))
    mixing = jnp.dot(gram, basis, precision=lax.Precision.HIGHEST) / (trace / CKPTS + 1e-06)
    keep = (jnp.arange(COMPONENTS) < components[0]).astype(jnp.float32)

    def slab_loadings(index):
        centred = slab_centred(logprob_all, index)
        mixed = jnp.einsum('ctv,ck->ktv', centred, mixing, precision=lax.Precision.HIGHEST) / CKPTS
        return (mixed * keep[:, None, None]).astype(jnp.bfloat16)
    pieces = lax.map(slab_loadings, slab_index)
    loadings = jnp.transpose(pieces, (1, 0, 2, 3)).reshape(COMPONENTS, TOKENS, V)
    return (loadings, gram, target_logprob)
```

```python
import functools

import jax
import jax.numpy as jnp
from jax import lax
from jax.experimental import pallas as pl
from jax.experimental.pallas import tpu as pltpu
from jax.sharding import PartitionSpec as P

COMPONENTS = 8
LANES = 128
MESH = pl.DeviceIdType.MESH
LOW = -1e30
NT = (((1,), (1,)), ((), ()))
RING = 4
STEPS = 2
HOLD = 4


def split_tiles(width):
    tiles = -(-width // LANES)
    best = tiles
    for per in range(1, tiles + 1):
        if tiles % per == 0 and per >= 6:
            best = per
            break
    return best * LANES, tiles // best


def spread_steps(steps_ref, shape):
    lane_owner = lax.broadcasted_iota(jnp.int32, shape, 1) % steps_ref.shape[0]
    out = jnp.zeros(shape, jnp.float32)
    for c in range(steps_ref.shape[0]):
        out = jnp.where(lane_owner == c, steps_ref[c].astype(jnp.float32), out)
    return out


def halves(value):
    high = value.astype(jnp.bfloat16)
    return high, (value - high.astype(jnp.float32)).astype(jnp.bfloat16)


def select_sum(value, table):
    count = value.shape[0]
    both = jnp.dot(
        jnp.concatenate(halves(value), axis=0), table, preferred_element_type=jnp.float32
    )
    return both[:count] + both[count:]


def gather_kernel(
    sizes,
    hidden_hbm, gain_hbm, bias_hbm, ids_hbm, steps_hbm, comps_hbm, w_hbm,
    xout_ref, w2_ref, gexp_ref, target_ref,
    normed, wbuf, xsend, xrecv, off, ids, tops, sums, hits, stat, stats, dsend, drecv,
    gsend, grecv, basis, to_flat, from_flat,
    hidden_ref, gain_ref, bias_ref, ids_ref, steps_ref, comps_ref, in_sem, wsem,
    send_sem, recv_sem, ssend, srecv, dssem, drsem, gssem, grsem, out_sem,
):
    owners, shards, tokens, width, tile, chunks = sizes
    slab = tokens // owners
    rows = owners * slab
    kinds = COMPONENTS
    ring = wbuf.shape[0]
    cut = (tile // LANES // 3) * LANES
    flats = gsend.shape[1]
    me = lax.axis_index("ckpt")
    mine = lax.axis_index("vocab")
    my_rows = pl.ds(pl.multiple_of(me * slab, slab), slab)
    last = chunks - 1
    last_rows = width - last * tile

    def peer(r):
        return lax.rem(me + r, owners)

    def side(r):
        return lax.rem(mine + r, shards)

    def iota(shape, axis):
        return lax.broadcasted_iota(jnp.int32, shape, axis)

    def fetch(j, slot, begin=0, count=None, sem=None):
        count = tile if count is None else count
        start = j * tile + begin
        return pltpu.make_async_copy(
            w_hbm.at[pl.ds(start if isinstance(start, int) else pl.multiple_of(start, LANES), count), :],
            wbuf.at[slot, pl.ds(begin, count), :],
            wsem.at[slot if sem is None else sem],
        )

    loads = []
    for i, (src, dst) in enumerate((
        (hidden_hbm, hidden_ref), (gain_hbm, gain_ref), (bias_hbm, bias_ref),
        (ids_hbm, ids_ref), (steps_hbm, steps_ref), (comps_hbm, comps_ref),
    )):
        loads.append(pltpu.make_async_copy(src, dst, in_sem.at[i]))
    for load in loads[:3]:
        load.start()
    fetch(0, 0, 0, cut).start()
    barrier = pltpu.get_barrier_semaphore()
    for q in range(shards - 1, -1, -1):
        for r in range(owners - 1, -1, -1):
            if q or r:
                pl.semaphore_signal(
                    barrier, inc=1, device_id=(peer(r), side(q)), device_id_type=MESH
                )
    fetch(0, 0, cut, tile - cut, ring).start()
    for load in loads[3:]:
        load.start()
    for j in range(1, ring):
        if j == last:
            fetch(j, j % ring, 0, last_rows).start()
        elif j < last:
            fetch(j, j % ring).start()
    for load in loads[:3]:
        load.wait()
    floats = hidden_ref[...].astype(jnp.float32)
    centre = jnp.mean(floats, axis=1, keepdims=True)
    spread = jnp.mean((floats - centre) ** 2, axis=1, keepdims=True)
    normed[...] = (
        (floats - centre) / jnp.sqrt(spread + 1e-05) * gain_ref[...] + bias_ref[...]
    ).astype(jnp.bfloat16)
    lane = iota((tokens, LANES), 1)

    def columns(start, count):
        return pl.ds(start if isinstance(start, int) else pl.multiple_of(start, LANES), count)

    def logits_of(slot, begin, count):
        return lax.dot_general(
            normed[...], wbuf[slot, pl.ds(begin, count), :], NT,
            preferred_element_type=jnp.float32,
        )

    def split_parts(logits, start, edge):
        parts = []
        for g in range(logits.shape[1] // LANES):
            part = logits[:, g * LANES:(g + 1) * LANES]
            inside = None
            if edge and start + (g + 1) * LANES > width:
                inside = (start + g * LANES + lane) < width
            parts.append((part, inside))
        return parts

    def store(parts, start):
        shift = off[...]
        for g, (part, inside) in enumerate(parts):
            value = part - shift
            if inside is not None:
                value = jnp.where(inside, value, 0.0)
            xsend[:, columns(start + g * LANES, LANES)] = value.astype(jnp.bfloat16)

    def send(start, count, piece):
        for r in range(1, owners):
            to = peer(r)
            pltpu.make_async_remote_copy(
                src_ref=xsend.at[
                    pl.ds(pl.multiple_of(to * slab, slab), slab), columns(start, count)
                ],
                dst_ref=xrecv.at[my_rows, columns(start, count)],
                send_sem=send_sem.at[r],
                recv_sem=recv_sem.at[piece],
                device_id=(to, mine),
                device_id_type=MESH,
            ).start()
        pltpu.make_async_copy(
            xsend.at[my_rows, columns(start, count)],
            xrecv.at[my_rows, columns(start, count)],
            recv_sem.at[piece],
        ).start()

    def gather_stats(parts, start):
        old_top = tops[...]
        new_top = old_top
        kept = []
        for part, inside in parts:
            if inside is not None:
                part = jnp.where(inside, part, LOW)
            kept.append(part)
            new_top = jnp.maximum(new_top, part)
        acc = sums[...] * jnp.exp(old_top - new_top)
        hit = hits[...]
        wanted = ids[...] - (mine * width + start)
        for g, (part, inside) in enumerate(parts):
            acc = acc + jnp.exp(kept[g] - new_top)
            match = (g * LANES + lane) == wanted
            if inside is not None:
                match = match & inside
            hit = hit + jnp.where(match, part, 0.0)
        tops[...] = new_top
        sums[...] = acc
        hits[...] = hit

    fetch(0, 0, 0, cut).wait()
    logits = logits_of(0, 0, cut)
    total = logits[:, :LANES]
    for g in range(1, cut // LANES):
        total = total + logits[:, g * LANES:(g + 1) * LANES]
    off[...] = jnp.broadcast_to(
        jnp.sum(total, axis=1, keepdims=True) * (1.0 / cut), off.shape
    )
    parts = split_parts(logits, 0, False)
    store(parts, 0)
    pl.semaphore_wait(barrier, owners * shards - 1)
    send(0, cut, 0)
    for load in loads[3:]:
        load.wait()
    wide = jnp.broadcast_to(ids_ref[...].astype(jnp.float32), (LANES, tokens))
    ids[...] = jnp.transpose(wide).astype(jnp.int32)
    tops[...] = jnp.full_like(tops, LOW)
    sums[...] = jnp.zeros_like(sums)
    hits[...] = jnp.zeros_like(hits)

    fetch(0, 0, cut, tile - cut, ring).wait()
    more = logits_of(0, cut, tile - cut)
    more_parts = split_parts(more, cut, False)
    store(more_parts, cut)
    send(cut, tile - cut, 1)
    gather_stats(parts, 0)
    gather_stats(more_parts, cut)
    if ring == last:
        fetch(last, 0, 0, last_rows).start()
    elif ring < last:
        fetch(ring, 0).start()

    held = max(1, last - HOLD)

    def middle(j, carry):
        slot = lax.rem(j, ring)
        start = j * tile
        fetch(j, slot).wait()
        chunk_parts = split_parts(logits_of(slot, 0, tile), start, False)
        store(chunk_parts, start)

        @pl.when(j < held)
        def _():
            send(start, tile, j + 1)

        gather_stats(chunk_parts, start)

        @pl.when(j + ring < last)
        def _():
            fetch(j + ring, slot).start()

        @pl.when(j + ring == last)
        def _():
            fetch(last, slot, 0, last_rows).start()

        return carry

    lax.fori_loop(1, last, middle, 0)
    tail_at = last * tile
    fetch(last, last % ring, 0, last_rows).wait()
    tail_parts = split_parts(logits_of(last % ring, 0, tile), tail_at, True)
    store(tail_parts, tail_at)
    gather_stats(tail_parts, tail_at)

    top = jnp.max(tops[...], axis=1, keepdims=True)
    total = jnp.sum(sums[...] * jnp.exp(tops[...] - top), axis=1, keepdims=True)
    picked = jnp.sum(hits[...], axis=1, keepdims=True)
    stat[...] = jnp.where(lane == 0, top, jnp.where(lane == 1, total, picked))
    sent = []
    for r in range(1, shards):
        copy = pltpu.make_async_remote_copy(
            src_ref=stat,
            dst_ref=stats.at[r - 1],
            send_sem=ssend.at[r - 1],
            recv_sem=srecv.at[r - 1],
            device_id=(me, side(r)),
            device_id_type=MESH,
        )
        copy.start()
        sent.append(copy)

    to_flat[...] = (iota((rows, flats), 0) // slab == iota((rows, flats), 1) % owners).astype(
        jnp.bfloat16
    )
    from_flat[...] = (
        iota((flats, rows), 0) % owners == iota((flats, rows), 1) // slab
    ).astype(jnp.bfloat16)
    at_steps = spread_steps(steps_ref, (kinds, LANES))
    cosines = jnp.cos(
        jnp.pi * (iota((kinds, LANES), 0) + 1).astype(jnp.float32) * at_steps / 143000.0
    )
    level = jnp.sum(
        jnp.where(iota((kinds, LANES), 1) < owners, cosines, 0.0), axis=1, keepdims=True
    ) * (1.0 / owners)
    for d in range(owners):
        basis[d] = jnp.broadcast_to(cosines[:, d:d + 1] - level, (kinds, rows))

    for copy in sent:
        copy.wait()
    best = top
    for r in range(shards - 1):
        best = jnp.maximum(best, stats[r][:, 0:1])
    total = total * jnp.exp(top - best)
    for r in range(shards - 1):
        total = total + stats[r][:, 1:2] * jnp.exp(stats[r][:, 0:1] - best)
        picked = picked + stats[r][:, 2:3]
    lse = best + jnp.log(total)
    dsend[...] = jnp.broadcast_to(off[:, 0:1] - lse, dsend.shape)
    for r in range(1, owners):
        to = peer(r)
        pltpu.make_async_remote_copy(
            src_ref=dsend.at[pl.ds(pl.multiple_of(to * slab, slab), slab), :],
            dst_ref=drecv.at[my_rows, :],
            send_sem=dssem.at[0],
            recv_sem=drsem.at[0],
            device_id=(to, mine),
            device_id_type=MESH,
        ).start()
    pltpu.make_async_copy(dsend.at[my_rows, :], drecv.at[my_rows, :], drsem.at[0]).start()

    def late(j, carry):
        send(j * tile, tile, j + 1)
        return carry

    lax.fori_loop(held, last, late, 0)
    send(tail_at, tile - cut, chunks)
    send(tail_at + tile - cut, cut, chunks + 1)
    target_ref[...] = jnp.transpose(
        jnp.broadcast_to(picked - lse, (tokens, LANES))
    )[0:1, :]

    pltpu.make_async_copy(drecv, drecv, drsem.at[0]).wait()
    d = drecv[...].reshape(owners, slab, LANES)
    d = d - jnp.mean(d, axis=0, keepdims=True)
    drecv[...] = d.reshape(rows, LANES)

    def absorb(start, count, piece, products, edge=False):
        block = xrecv.at[:, columns(start, count)]
        pltpu.make_async_copy(block, block, recv_sem.at[piece]).wait()
        level = drecv[...].reshape(owners, slab, LANES)
        for g in range(count // LANES):
            at = columns(start + g * LANES, LANES)
            x = xrecv[:, at].astype(jnp.float32).reshape(owners, slab, LANES)
            x = x - jnp.mean(x, axis=0, keepdims=True) + level
            if edge and start + (g + 1) * LANES > width:
                x = jnp.where(start + g * LANES + iota(x.shape, 2) < width, x, 0.0)
            xrecv[:, at] = x.reshape(rows, LANES).astype(jnp.bfloat16)
        kept = xrecv[:, columns(start, count)]
        pltpu.make_async_copy(block, xout_ref.at[:, columns(start, count)], out_sem.at[0]).start()
        return products + lax.dot_general(kept, kept, NT, preferred_element_type=jnp.float32)

    products = absorb(0, cut, 0, jnp.zeros((rows, rows), jnp.float32))
    products = absorb(cut, tile - cut, 1, products)
    products = lax.fori_loop(
        1, last, lambda j, p: absorb(j * tile, tile, j + 1, p), products
    )
    products = absorb(tail_at, tile - cut, chunks, products, True)
    products = absorb(tail_at + tile - cut, cut, chunks + 1, products, True)

    matched = iota((rows, rows), 0) % slab == iota((rows, rows), 1) % slab
    partial = jnp.sum(
        jnp.where(matched, products, 0.0).reshape(owners, slab, rows), axis=1
    )
    flat_own = iota((owners, flats), 1) // owners == iota((owners, flats), 0)
    gsend[...] = jnp.sum(
        jnp.where(flat_own, select_sum(partial, to_flat[...]), 0.0), axis=0, keepdims=True
    )
    slot = mine * owners + me
    for q in range(shards - 1, -1, -1):
        for r in range(owners - 1, -1, -1):
            if q or r:
                pltpu.make_async_remote_copy(
                    src_ref=gsend,
                    dst_ref=grecv.at[slot],
                    send_sem=gssem.at[0],
                    recv_sem=grsem.at[0],
                    device_id=(peer(r), side(q)),
                    device_id_type=MESH,
                ).start()
    pltpu.make_async_copy(gsend, grecv.at[slot], grsem.at[0]).start()
    for r in range(1, owners):
        strip = xsend.at[my_rows, :]
        pltpu.make_async_copy(strip, strip, send_sem.at[r]).wait()
    others = pl.ds(0, rows - slab)
    pltpu.make_async_copy(dsend.at[others, :], dsend.at[others, :], dssem.at[0]).wait()
    row_k = iota((kinds, slab, rows), 0)
    keep = (iota((kinds, slab, rows), 2) % slab == iota((kinds, slab, rows), 1)) & (
        row_k < comps_ref[0]
    )
    flat_diag = iota((1, flats), 1) // owners == iota((1, flats), 1) % owners

    pltpu.make_async_copy(grecv, grecv, grsem.at[0]).wait()
    flat = jnp.sum(grecv[...], axis=0) * (1.0 / (tokens * width * shards))
    trace = jnp.sum(jnp.where(flat_diag, flat, 0.0), axis=1, keepdims=True)
    gexp = select_sum(
        jnp.where(flat_own, jnp.broadcast_to(flat, flat_own.shape), 0.0), from_flat[...]
    )
    mixed = basis[0] * gexp[0:1, :]
    for d in range(1, owners):
        mixed = mixed + basis[d] * gexp[d:d + 1, :]
    mixed = mixed * (1.0 / (trace * (1.0 / owners) + 1e-06) * (1.0 / owners))
    spreadout = jnp.where(
        keep, jnp.broadcast_to(mixed.reshape(kinds, 1, rows), keep.shape), 0.0
    ).reshape(kinds * slab, rows)
    high, low = halves(spreadout)
    w2_ref[:, 0:rows] = high
    w2_ref[:, rows:] = low
    gexp_ref[...] = gexp
    pltpu.make_async_copy(xrecv, xout_ref.at[:, columns(0, tile * chunks)], out_sem.at[0]).wait()
    less = pl.ds(0, owners * shards - 1)
    pltpu.make_async_copy(grecv.at[less], grecv.at[less], gssem.at[0]).wait()


def mix_kernel(across, x_ref, w2_ref, gexp_ref, target_in, out_ref, gram_ref, target_ref):
    start = pl.multiple_of(pl.program_id(0) * across, LANES)
    x = x_ref[:, pl.ds(start, across)]
    out_ref[...] = jnp.dot(
        w2_ref[...], jnp.concatenate([x, x], axis=0), preferred_element_type=jnp.float32
    ).astype(jnp.bfloat16)

    @pl.when(pl.program_id(0) == pl.num_programs(0) - 1)
    def _():
        owners, rows = gexp_ref.shape
        pick = (
            lax.broadcasted_iota(jnp.int32, (rows, LANES), 0)
            == lax.broadcasted_iota(jnp.int32, (rows, LANES), 1) * (rows // owners)
        ).astype(jnp.float32)
        gram_ref[...] = jnp.dot(
            gexp_ref[...], pick, precision=lax.Precision.HIGHEST,
            preferred_element_type=jnp.float32,
        )[:, :owners]
        target_ref[...] = target_in[...]


def per_device(owners, shards, hidden_rows, norm_gain, norm_bias, unembed, target_ids, ckpt_steps, components):
    tokens, depth = hidden_rows.shape[1:]
    width = unembed.shape[2]
    slab = tokens // owners
    rows = owners * slab
    out_rows = COMPONENTS * slab
    tile, chunks = split_tiles(width)
    padded = tile * chunks
    across = -(-(padded // LANES) // STEPS) * LANES
    flats = max(owners * owners, LANES)
    ring = min(RING, chunks)
    sizes = (owners, shards, tokens, width, tile, chunks)
    f32, bf16 = jnp.float32, jnp.bfloat16
    vmem = pl.BlockSpec(memory_space=pltpu.VMEM)
    hbm = pl.BlockSpec(memory_space=pltpu.HBM)
    dma = pltpu.SemaphoreType.DMA
    limit = 67043328 - min(depth * width * 2 - (1 << 20), 16 << 20)

    def far(a):
        return pltpu.with_memory_space_constraint(a, pltpu.HBM)

    x, w2, gexp, target = pl.pallas_call(
        functools.partial(gather_kernel, sizes),
        in_specs=[hbm] * 7,
        out_specs=[pl.BlockSpec(memory_space=pl.ANY), vmem, vmem, vmem],
        out_shape=[
            jax.ShapeDtypeStruct((rows, across * STEPS), bf16),
            jax.ShapeDtypeStruct((out_rows, 2 * rows), bf16),
            jax.ShapeDtypeStruct((owners, rows), f32),
            jax.ShapeDtypeStruct((1, tokens), f32),
        ],
        scratch_shapes=[
            pltpu.VMEM((tokens, depth), bf16),
            pltpu.VMEM((ring, tile, depth), bf16),
            pltpu.VMEM((tokens, padded), bf16),
            pltpu.VMEM((rows, padded), bf16),
            pltpu.VMEM((tokens, LANES), f32),
            pltpu.VMEM((tokens, LANES), jnp.int32),
            pltpu.VMEM((tokens, LANES), f32),
            pltpu.VMEM((tokens, LANES), f32),
            pltpu.VMEM((tokens, LANES), f32),
            pltpu.VMEM((tokens, LANES), f32),
            pltpu.VMEM((shards - 1, tokens, LANES), f32),
            pltpu.VMEM((tokens, LANES), f32),
            pltpu.VMEM((rows, LANES), f32),
            pltpu.VMEM((1, flats), f32),
            pltpu.VMEM((owners * shards, 1, flats), f32),
            pltpu.VMEM((owners, COMPONENTS, rows), f32),
            pltpu.VMEM((rows, flats), bf16),
            pltpu.VMEM((flats, rows), bf16),
            pltpu.VMEM((tokens, depth), bf16),
            pltpu.VMEM((1, depth), f32),
            pltpu.VMEM((1, depth), f32),
            pltpu.VMEM((1, tokens), jnp.int32),
            pltpu.SMEM((owners,), jnp.int32),
            pltpu.SMEM((1,), jnp.int32),
            dma((6,)), dma((ring + 1,)),
            dma((owners,)), dma((chunks + 2,)),
            dma((shards - 1,)), dma((shards - 1,)),
            dma((1,)), dma((1,)), dma((1,)), dma((1,)), dma((1,)),
        ],
        compiler_params=pltpu.CompilerParams(
            collective_id=0, has_side_effects=True, vmem_limit_bytes=limit,
        ),
    )(
        far(hidden_rows[0]), far(norm_gain), far(norm_bias),
        far(target_ids.reshape(1, tokens)), far(ckpt_steps), components, far(unembed[0].T),
    )

    out, gram, target = pl.pallas_call(
        functools.partial(mix_kernel, across),
        grid=(STEPS,),
        in_specs=[vmem] * 4,
        out_specs=[pl.BlockSpec((out_rows, across), lambda j: (0, j)), vmem, vmem],
        out_shape=[
            jax.ShapeDtypeStruct((out_rows, width), bf16),
            jax.ShapeDtypeStruct((owners, owners), f32),
            jax.ShapeDtypeStruct((1, tokens), f32),
        ],
        compiler_params=pltpu.CompilerParams(
            dimension_semantics=("arbitrary",),
            vmem_limit_bytes=rows * across * STEPS * 2 + 12 * out_rows * across + (8 << 20),
        ),
    )(x, w2, gexp, target)
    return out.reshape(COMPONENTS, slab, width), gram, target


def solution(mesh):
    return jax.shard_map(
        functools.partial(per_device, mesh.shape["ckpt"], mesh.shape["vocab"]),
        mesh=mesh,
        in_specs=(
            P("ckpt", None, None),
            P("ckpt", None),
            P("ckpt", None),
            P("ckpt", None, "vocab"),
            P(),
            P(),
            P(),
        ),
        out_specs=(P(None, "ckpt", "vocab"), P(), P("ckpt", None)),
        check_vma=False,
    )
```

```python
import functools

import jax
import jax.numpy as jnp
from jax import lax
from jax.experimental import pallas as pl
from jax.experimental.pallas import tpu as pltpu
from jax.sharding import PartitionSpec as P

COMPONENTS = 8
LANES = 128
MESH = pl.DeviceIdType.MESH
LOW = -1e30
NT = (((1,), (1,)), ((), ()))
RING = 4
STEPS = 2
HOLD = 2


def split_tiles(width):
    tiles = -(-width // LANES)
    best = tiles
    for per in range(1, tiles + 1):
        if tiles % per == 0 and per >= 6:
            best = per
            break
    return best * LANES, tiles // best


def spread_steps(steps_ref, shape):
    lane_owner = lax.broadcasted_iota(jnp.int32, shape, 1) % steps_ref.shape[0]
    out = jnp.zeros(shape, jnp.float32)
    for c in range(steps_ref.shape[0]):
        out = jnp.where(lane_owner == c, steps_ref[c].astype(jnp.float32), out)
    return out


def halves(value):
    high = value.astype(jnp.bfloat16)
    return high, (value - high.astype(jnp.float32)).astype(jnp.bfloat16)


def select_sum(value, table):
    count = value.shape[0]
    both = jnp.dot(
        jnp.concatenate(halves(value), axis=0), table, preferred_element_type=jnp.float32
    )
    return both[:count] + both[count:]


def gather_kernel(
    sizes,
    hidden_hbm, gain_hbm, bias_hbm, ids_hbm, steps_hbm, comps_ref, w_hbm,
    xout_ref, w2_ref, gexp_ref, target_ref,
    normed, wbuf, xsend, xrecv, off, ids, tops, sums, hits, stat, stats, dsend, drecv, dcol,
    gsend, grecv, basis, to_flat, from_flat,
    hidden_ref, gain_ref, bias_ref, ids_ref, steps_ref, in_sem, wsem,
    send_sem, recv_sem, ssend, srecv, dssem, drsem, gssem, grsem, out_sem, ready,
):
    owners, shards, tokens, width, tile, chunks = sizes
    slab = tokens // owners
    rows = owners * slab
    kinds = COMPONENTS
    ring = wbuf.shape[0]
    cut = (tile // LANES // 3) * LANES
    flats = gsend.shape[1]
    me = lax.axis_index("ckpt")
    mine = lax.axis_index("vocab")
    my_rows = pl.ds(pl.multiple_of(me * slab, slab), slab)
    last = chunks - 1
    last_rows = width - last * tile

    def peer(r):
        return lax.rem(me + r, owners)

    def side(r):
        return lax.rem(mine + r, shards)

    def iota(shape, axis):
        return lax.broadcasted_iota(jnp.int32, shape, axis)

    def fetch(j, slot, begin=0, count=None, sem=None):
        count = tile if count is None else count
        start = j * tile + begin
        return pltpu.make_async_copy(
            w_hbm.at[pl.ds(start if isinstance(start, int) else pl.multiple_of(start, LANES), count), :],
            wbuf.at[slot, pl.ds(begin, count), :],
            wsem.at[slot if sem is None else sem],
        )

    loads = []
    for i, (src, dst) in enumerate((
        (hidden_hbm, hidden_ref), (gain_hbm, gain_ref), (bias_hbm, bias_ref),
        (ids_hbm, ids_ref), (steps_hbm, steps_ref),
    )):
        loads.append(pltpu.make_async_copy(src, dst, in_sem.at[i]))
    for load in loads[:3]:
        load.start()
    fetch(0, 0, 0, cut).start()
    barrier = pltpu.get_barrier_semaphore()
    greeted = [(0, q) for q in range(1, shards)] + [(r, 0) for r in range(1, owners)]
    for r, q in greeted:
        pl.semaphore_signal(
            barrier, inc=1, device_id=(peer(r), side(q)), device_id_type=MESH
        )
    fetch(0, 0, cut, tile - cut, ring).start()
    for load in loads[3:]:
        load.start()
    for j in range(1, ring):
        if j == last:
            fetch(j, j % ring, 0, last_rows).start()
        elif j < last:
            fetch(j, j % ring).start()
    for load in loads[:3]:
        load.wait()
    floats = hidden_ref[...].astype(jnp.float32)
    centre = jnp.mean(floats, axis=1, keepdims=True)
    spread = jnp.mean((floats - centre) ** 2, axis=1, keepdims=True)
    normed[...] = (
        (floats - centre) * (1.0 / jnp.sqrt(spread + 1e-05)) * gain_ref[...] + bias_ref[...]
    ).astype(jnp.bfloat16)
    lane = iota((tokens, LANES), 1)

    def columns(start, count):
        return pl.ds(start if isinstance(start, int) else pl.multiple_of(start, LANES), count)

    def logits_of(slot, begin, count):
        return lax.dot_general(
            normed[...], wbuf[slot, pl.ds(begin, count), :], NT,
            preferred_element_type=jnp.float32,
        )

    def split_parts(logits, start, edge):
        parts = []
        for g in range(logits.shape[1] // LANES):
            part = logits[:, g * LANES:(g + 1) * LANES]
            inside = None
            if edge and start + (g + 1) * LANES > width:
                inside = (start + g * LANES + lane) < width
            parts.append((part, inside))
        return parts

    def store(parts, start):
        shift = off[...]
        for g, (part, inside) in enumerate(parts):
            value = part - shift
            if inside is not None:
                value = jnp.where(inside, value, 0.0)
            xsend[:, columns(start + g * LANES, LANES)] = value.astype(jnp.bfloat16)

    def send(start, count, piece):
        for r in range(1, owners):
            to = peer(r)
            pltpu.make_async_remote_copy(
                src_ref=xsend.at[
                    pl.ds(pl.multiple_of(to * slab, slab), slab), columns(start, count)
                ],
                dst_ref=xrecv.at[my_rows, columns(start, count)],
                send_sem=send_sem.at[r],
                recv_sem=recv_sem.at[piece],
                device_id=(to, mine),
                device_id_type=MESH,
            ).start()
        pltpu.make_async_copy(
            xsend.at[my_rows, columns(start, count)],
            xrecv.at[my_rows, columns(start, count)],
            recv_sem.at[piece],
        ).start()

    def gather_stats(parts, start):
        old_top = tops[...]
        new_top = old_top
        kept = []
        for part, inside in parts:
            if inside is not None:
                part = jnp.where(inside, part, LOW)
            kept.append(part)
            new_top = jnp.maximum(new_top, part)
        acc = sums[...] * jnp.exp(old_top - new_top)
        hit = hits[...]
        wanted = ids[...] - (mine * width + start)
        for g, (part, inside) in enumerate(parts):
            acc = acc + jnp.exp(kept[g] - new_top)
            match = (g * LANES + lane) == wanted
            if inside is not None:
                match = match & inside
            hit = hit + jnp.where(match, part, 0.0)
        tops[...] = new_top
        sums[...] = acc
        hits[...] = hit

    fetch(0, 0, 0, cut).wait()
    logits = logits_of(0, 0, cut)
    total = logits[:, :LANES]
    for g in range(1, cut // LANES):
        total = total + logits[:, g * LANES:(g + 1) * LANES]
    off[...] = jnp.broadcast_to(
        jnp.sum(total, axis=1, keepdims=True) * (1.0 / cut), off.shape
    )
    parts = split_parts(logits, 0, False)
    store(parts, 0)
    pl.semaphore_wait(barrier, owners + shards - 2)
    send(0, cut, 0)
    for r in range(1, owners):
        pl.semaphore_signal(ready, inc=1, device_id=(peer(r), mine), device_id_type=MESH)
    for load in loads[3:]:
        load.wait()
    wide = jnp.broadcast_to(ids_ref[...].astype(jnp.float32), (LANES, tokens))
    ids[...] = jnp.transpose(wide).astype(jnp.int32)
    tops[...] = jnp.full_like(tops, LOW)
    sums[...] = jnp.zeros_like(sums)
    hits[...] = jnp.zeros_like(hits)

    fetch(0, 0, cut, tile - cut, ring).wait()
    more = logits_of(0, cut, tile - cut)
    more_parts = split_parts(more, cut, False)
    store(more_parts, cut)
    send(cut, tile - cut, 1)
    gather_stats(parts, 0)
    gather_stats(more_parts, cut)
    if ring == last:
        fetch(last, 0, 0, last_rows).start()
    elif ring < last:
        fetch(ring, 0).start()

    held = max(1, last - HOLD)

    def middle(j, carry):
        slot = lax.rem(j, ring)
        start = j * tile
        fetch(j, slot).wait()
        chunk_parts = split_parts(logits_of(slot, 0, tile), start, False)
        store(chunk_parts, start)

        @pl.when(j < held)
        def _():
            send(start, tile, j + 1)

        gather_stats(chunk_parts, start)

        @pl.when(j + ring < last)
        def _():
            fetch(j + ring, slot).start()

        @pl.when(j + ring == last)
        def _():
            fetch(last, slot, 0, last_rows).start()

        return carry

    lax.fori_loop(1, last, middle, 0)
    tail_at = last * tile
    fetch(last, last % ring, 0, last_rows).wait()
    tail_parts = split_parts(logits_of(last % ring, 0, tile), tail_at, True)
    store(tail_parts, tail_at)
    gather_stats(tail_parts, tail_at)

    top = jnp.max(tops[...], axis=1, keepdims=True)
    total = jnp.sum(sums[...] * jnp.exp(tops[...] - top), axis=1, keepdims=True)
    picked = jnp.sum(hits[...], axis=1, keepdims=True)
    stat[...] = jnp.transpose(
        jnp.where(
            lane == 0, top,
            jnp.where(lane == 1, total, jnp.where(lane == 2, picked, off[...])),
        )
    )[0:8, :]
    sent = []
    for r in range(1, shards):
        copy = pltpu.make_async_remote_copy(
            src_ref=stat,
            dst_ref=stats.at[r - 1],
            send_sem=ssend.at[r - 1],
            recv_sem=srecv.at[r - 1],
            device_id=(me, side(r)),
            device_id_type=MESH,
        )
        copy.start()
        sent.append(copy)

    to_flat[...] = (iota((rows, flats), 0) // slab == iota((rows, flats), 1) % owners).astype(
        jnp.bfloat16
    )
    from_flat[...] = (
        iota((flats, rows), 0) % owners == iota((flats, rows), 1) // slab
    ).astype(jnp.bfloat16)
    at_steps = spread_steps(steps_ref, (kinds, LANES))
    cosines = jnp.cos(
        jnp.pi * (iota((kinds, LANES), 0) + 1).astype(jnp.float32) * at_steps / 143000.0
    )
    level = jnp.sum(
        jnp.where(iota((kinds, LANES), 1) < owners, cosines, 0.0), axis=1, keepdims=True
    ) * (1.0 / owners)
    for d in range(owners):
        basis[d] = jnp.broadcast_to(cosines[:, d:d + 1] - level, (kinds, rows))

    for copy in sent:
        copy.wait()
    best = stat[0:1, :]
    for r in range(shards - 1):
        best = jnp.maximum(best, stats[r][0:1, :])
    total = stat[1:2, :] * jnp.exp(stat[0:1, :] - best)
    picked = stat[2:3, :]
    for r in range(shards - 1):
        total = total + stats[r][1:2, :] * jnp.exp(stats[r][0:1, :] - best)
        picked = picked + stats[r][2:3, :]
    lse = best + jnp.log(total)
    dsend[...] = stat[3:4, :] - lse
    for r in range(1, owners):
        pltpu.make_async_remote_copy(
            src_ref=dsend,
            dst_ref=drecv.at[me],
            send_sem=dssem.at[0],
            recv_sem=drsem.at[0],
            device_id=(peer(r), mine),
            device_id_type=MESH,
        ).start()
    pltpu.make_async_copy(dsend, drecv.at[me], drsem.at[0]).start()

    def late(j, carry):
        send(j * tile, tile, j + 1)
        return carry

    lax.fori_loop(held, last, late, 0)
    send(tail_at, tile - cut, chunks)
    send(tail_at + tile - cut, cut, chunks + 1)
    target_ref[...] = picked - lse

    pltpu.make_async_copy(drecv, drecv, drsem.at[0]).wait()
    d = drecv[...]
    d = jnp.broadcast_to(d - jnp.mean(d, axis=0, keepdims=True), (owners, slab, tokens))
    here = iota(d.shape, 2) == me * slab + iota(d.shape, 1)
    d = jnp.sum(jnp.where(here, d, 0.0), axis=2, keepdims=True)
    dcol[...] = jnp.broadcast_to(d, (owners, slab, LANES)).reshape(rows, LANES)

    def absorb(start, count, piece, products, edge=False):
        block = xrecv.at[:, columns(start, count)]
        pltpu.make_async_copy(block, block, recv_sem.at[piece]).wait()
        level = dcol[...].reshape(owners, slab, LANES)
        for g in range(count // LANES):
            at = columns(start + g * LANES, LANES)
            x = xrecv[:, at].astype(jnp.float32).reshape(owners, slab, LANES)
            x = x - jnp.mean(x, axis=0, keepdims=True) + level
            if edge and start + (g + 1) * LANES > width:
                x = jnp.where(start + g * LANES + iota(x.shape, 2) < width, x, 0.0)
            xrecv[:, at] = x.reshape(rows, LANES).astype(jnp.bfloat16)
        kept = xrecv[:, columns(start, count)]
        pltpu.make_async_copy(block, xout_ref.at[:, columns(start, count)], out_sem.at[0]).start()
        return products + lax.dot_general(kept, kept, NT, preferred_element_type=jnp.float32)

    products = absorb(0, cut, 0, jnp.zeros((rows, rows), jnp.float32))
    products = absorb(cut, tile - cut, 1, products)
    products = lax.fori_loop(
        1, last, lambda j, p: absorb(j * tile, tile, j + 1, p), products
    )
    products = absorb(tail_at, tile - cut, chunks, products, True)
    products = absorb(tail_at + tile - cut, cut, chunks + 1, products, True)

    matched = iota((rows, rows), 0) % slab == iota((rows, rows), 1) % slab
    partial = jnp.sum(
        jnp.where(matched, products, 0.0).reshape(owners, slab, rows), axis=1
    )
    flat_own = iota((owners, flats), 1) // owners == iota((owners, flats), 0)
    gsend[...] = jnp.sum(
        jnp.where(flat_own, select_sum(partial, to_flat[...]), 0.0), axis=0, keepdims=True
    )
    slot = mine * owners + me
    pl.semaphore_wait(ready, owners - 1)
    for q in range(shards):
        for r in range(owners):
            @pl.when(slot != q * owners + r)
            def _(q=q, r=r):
                pltpu.make_async_remote_copy(
                    src_ref=gsend,
                    dst_ref=grecv.at[slot],
                    send_sem=gssem.at[0],
                    recv_sem=grsem.at[0],
                    device_id=(jnp.int32(r), jnp.int32(q)),
                    device_id_type=MESH,
                ).start()

    pltpu.make_async_copy(gsend, grecv.at[slot], grsem.at[0]).start()
    for r in range(1, owners):
        strip = xsend.at[my_rows, :]
        pltpu.make_async_copy(strip, strip, send_sem.at[r]).wait()
    others = pl.ds(0, owners - 1)
    pltpu.make_async_copy(drecv.at[others], drecv.at[others], dssem.at[0]).wait()
    row_k = iota((kinds, slab, rows), 0)
    keep = (iota((kinds, slab, rows), 2) % slab == iota((kinds, slab, rows), 1)) & (
        row_k < comps_ref[0]
    )
    flat_diag = iota((1, flats), 1) // owners == iota((1, flats), 1) % owners

    pltpu.make_async_copy(grecv, grecv, grsem.at[0]).wait()
    flat = jnp.sum(grecv[...], axis=0) * (1.0 / (tokens * width * shards))
    trace = jnp.sum(jnp.where(flat_diag, flat, 0.0), axis=1, keepdims=True)
    gexp = select_sum(
        jnp.where(flat_own, jnp.broadcast_to(flat, flat_own.shape), 0.0), from_flat[...]
    )
    mixed = basis[0] * gexp[0:1, :]
    for d in range(1, owners):
        mixed = mixed + basis[d] * gexp[d:d + 1, :]
    mixed = mixed * (1.0 / (trace * (1.0 / owners) + 1e-06) * (1.0 / owners))
    spreadout = jnp.where(
        keep, jnp.broadcast_to(mixed.reshape(kinds, 1, rows), keep.shape), 0.0
    ).reshape(kinds * slab, rows)
    high, low = halves(spreadout)
    w2_ref[:, 0:rows] = high
    w2_ref[:, rows:] = low
    gexp_ref[...] = gexp
    pltpu.make_async_copy(xrecv, xout_ref.at[:, columns(0, tile * chunks)], out_sem.at[0]).wait()
    less = pl.ds(0, owners * shards - 1)
    pltpu.make_async_copy(grecv.at[less], grecv.at[less], gssem.at[0]).wait()


def mix_kernel(across, x_ref, w2_ref, gexp_ref, target_in, out_ref, gram_ref, target_ref):
    start = pl.multiple_of(pl.program_id(0) * across, LANES)
    x = x_ref[:, pl.ds(start, across)]
    out_ref[...] = jnp.dot(
        w2_ref[...], jnp.concatenate([x, x], axis=0), preferred_element_type=jnp.float32
    ).astype(jnp.bfloat16)

    @pl.when(pl.program_id(0) == pl.num_programs(0) - 1)
    def _():
        owners, rows = gexp_ref.shape
        pick = (
            lax.broadcasted_iota(jnp.int32, (rows, LANES), 0)
            == lax.broadcasted_iota(jnp.int32, (rows, LANES), 1) * (rows // owners)
        ).astype(jnp.float32)
        gram_ref[...] = jnp.dot(
            gexp_ref[...], pick, precision=lax.Precision.HIGHEST,
            preferred_element_type=jnp.float32,
        )[:, :owners]
        target_ref[...] = target_in[...]


def per_device(owners, shards, hidden_rows, norm_gain, norm_bias, unembed, target_ids, ckpt_steps, components):
    tokens, depth = hidden_rows.shape[1:]
    width = unembed.shape[2]
    slab = tokens // owners
    rows = owners * slab
    out_rows = COMPONENTS * slab
    tile, chunks = split_tiles(width)
    padded = tile * chunks
    across = -(-(padded // LANES) // STEPS) * LANES
    flats = max(owners * owners, LANES)
    ring = min(RING, chunks)
    sizes = (owners, shards, tokens, width, tile, chunks)
    f32, bf16 = jnp.float32, jnp.bfloat16
    vmem = pl.BlockSpec(memory_space=pltpu.VMEM)
    hbm = pl.BlockSpec(memory_space=pltpu.HBM)
    dma = pltpu.SemaphoreType.DMA
    limit = 67043328 - min(depth * width * 2 - (1 << 20), 16 << 20)

    def far(a):
        return pltpu.with_memory_space_constraint(a, pltpu.HBM)

    x, w2, gexp, target = pl.pallas_call(
        functools.partial(gather_kernel, sizes),
        in_specs=[hbm] * 5 + [pl.BlockSpec(memory_space=pltpu.SMEM), hbm],
        out_specs=[pl.BlockSpec(memory_space=pl.ANY), vmem, vmem, vmem],
        out_shape=[
            jax.ShapeDtypeStruct((rows, across * STEPS), bf16),
            jax.ShapeDtypeStruct((out_rows, 2 * rows), bf16),
            jax.ShapeDtypeStruct((owners, rows), f32),
            jax.ShapeDtypeStruct((1, tokens), f32),
        ],
        scratch_shapes=[
            pltpu.VMEM((tokens, depth), bf16),
            pltpu.VMEM((ring, tile, depth), bf16),
            pltpu.VMEM((tokens, padded), bf16),
            pltpu.VMEM((rows, padded), bf16),
            pltpu.VMEM((tokens, LANES), f32),
            pltpu.VMEM((tokens, LANES), jnp.int32),
            pltpu.VMEM((tokens, LANES), f32),
            pltpu.VMEM((tokens, LANES), f32),
            pltpu.VMEM((tokens, LANES), f32),
            pltpu.VMEM((8, tokens), f32),
            pltpu.VMEM((shards - 1, 8, tokens), f32),
            pltpu.VMEM((1, tokens), f32),
            pltpu.VMEM((owners, 1, tokens), f32),
            pltpu.VMEM((rows, LANES), f32),
            pltpu.VMEM((1, flats), f32),
            pltpu.VMEM((owners * shards, 1, flats), f32),
            pltpu.VMEM((owners, COMPONENTS, rows), f32),
            pltpu.VMEM((rows, flats), bf16),
            pltpu.VMEM((flats, rows), bf16),
            pltpu.VMEM((tokens, depth), bf16),
            pltpu.VMEM((1, depth), f32),
            pltpu.VMEM((1, depth), f32),
            pltpu.VMEM((1, tokens), jnp.int32),
            pltpu.SMEM((owners,), jnp.int32),
            dma((5,)), dma((ring + 1,)),
            dma((owners,)), dma((chunks + 2,)),
            dma((shards - 1,)), dma((shards - 1,)),
            dma((1,)), dma((1,)), dma((1,)), dma((1,)), dma((1,)),
            pltpu.SemaphoreType.REGULAR,
        ],
        compiler_params=pltpu.CompilerParams(
            collective_id=0, has_side_effects=True, vmem_limit_bytes=limit,
        ),
    )(
        far(hidden_rows[0]), far(norm_gain), far(norm_bias),
        far(target_ids.reshape(1, tokens)), far(ckpt_steps), components, far(unembed[0].T),
    )

    out, gram, target = pl.pallas_call(
        functools.partial(mix_kernel, across),
        grid=(STEPS,),
        in_specs=[vmem] * 4,
        out_specs=[pl.BlockSpec((out_rows, across), lambda j: (0, j)), vmem, vmem],
        out_shape=[
            jax.ShapeDtypeStruct((out_rows, width), bf16),
            jax.ShapeDtypeStruct((owners, owners), f32),
            jax.ShapeDtypeStruct((1, tokens), f32),
        ],
        compiler_params=pltpu.CompilerParams(
            dimension_semantics=("arbitrary",),
            vmem_limit_bytes=rows * across * STEPS * 2 + 12 * out_rows * across + (8 << 20),
        ),
    )(x, w2, gexp, target)
    return out.reshape(COMPONENTS, slab, width), gram, target


def solution(mesh):
    return jax.shard_map(
        functools.partial(per_device, mesh.shape["ckpt"], mesh.shape["vocab"]),
        mesh=mesh,
        in_specs=(
            P("ckpt", None, None),
            P("ckpt", None),
            P("ckpt", None),
            P("ckpt", None, "vocab"),
            P(),
            P(),
            P(),
        ),
        out_specs=(P(None, "ckpt", "vocab"), P(), P("ckpt", None)),
        check_vma=False,
    )
```

```python
import functools

import jax
import jax.numpy as jnp
from jax import lax
from jax.experimental import pallas as pl
from jax.experimental.pallas import tpu as pltpu
from jax.sharding import PartitionSpec as P

COMPONENTS = 8
LANES = 128
MESH = pl.DeviceIdType.MESH
LOW = -1e30
NT = (((1,), (1,)), ((), ()))
RING = 4
HOLD = 2


def split_tiles(width):
    tiles = -(-width // LANES)
    best = tiles
    for per in range(1, tiles + 1):
        if tiles % per == 0 and per >= 6:
            best = per
            break
    return best * LANES, tiles // best


def spread_steps(steps_ref, shape):
    lane_owner = lax.broadcasted_iota(jnp.int32, shape, 1) % steps_ref.shape[0]
    out = jnp.zeros(shape, jnp.float32)
    for c in range(steps_ref.shape[0]):
        out = jnp.where(lane_owner == c, steps_ref[c].astype(jnp.float32), out)
    return out


def halves(value):
    high = value.astype(jnp.bfloat16)
    return high, (value - high.astype(jnp.float32)).astype(jnp.bfloat16)


def select_sum(value, table):
    count = value.shape[0]
    both = jnp.dot(
        jnp.concatenate(halves(value), axis=0), table, preferred_element_type=jnp.float32
    )
    return both[:count] + both[count:]


def gather_kernel(
    sizes,
    hidden_hbm, gain_hbm, bias_hbm, ids_hbm, steps_hbm, comps_ref, w_hbm,
    xout_ref, w2_ref, gexp_ref, target_ref,
    normed, wbuf, xsend, xrecv, off, ids, tops, sums, hits, stat, stats, dsend, drecv, dcol,
    gsend, grecv, basis, to_flat, from_flat,
    hidden_ref, gain_ref, bias_ref, ids_ref, steps_ref, in_sem, wsem,
    send_sem, recv_sem, ssend, srecv, dssem, drsem, gssem, grsem, out_sem, ready,
):
    owners, shards, tokens, width, tile, chunks = sizes
    slab = tokens // owners
    rows = owners * slab
    kinds = COMPONENTS
    ring = wbuf.shape[0]
    cut = (tile // LANES // 3) * LANES
    flats = gsend.shape[1]
    me = lax.axis_index("ckpt")
    mine = lax.axis_index("vocab")
    my_rows = pl.ds(pl.multiple_of(me * slab, slab), slab)
    last = chunks - 1
    last_rows = width - last * tile

    def peer(r):
        return lax.rem(me + r, owners)

    def side(r):
        return lax.rem(mine + r, shards)

    def iota(shape, axis):
        return lax.broadcasted_iota(jnp.int32, shape, axis)

    def fetch(j, slot, begin=0, count=None, sem=None):
        count = tile if count is None else count
        start = j * tile + begin
        return pltpu.make_async_copy(
            w_hbm.at[pl.ds(start if isinstance(start, int) else pl.multiple_of(start, LANES), count), :],
            wbuf.at[slot, pl.ds(begin, count), :],
            wsem.at[slot if sem is None else sem],
        )

    loads = []
    for i, (src, dst) in enumerate((
        (hidden_hbm, hidden_ref), (gain_hbm, gain_ref), (bias_hbm, bias_ref),
        (ids_hbm, ids_ref), (steps_hbm, steps_ref),
    )):
        loads.append(pltpu.make_async_copy(src, dst, in_sem.at[i]))
    for load in loads[:3]:
        load.start()
    fetch(0, 0, 0, cut).start()
    barrier = pltpu.get_barrier_semaphore()
    greeted = [(0, q) for q in range(1, shards)] + [(r, 0) for r in range(1, owners)]
    for r, q in greeted:
        pl.semaphore_signal(
            barrier, inc=1, device_id=(peer(r), side(q)), device_id_type=MESH
        )
    fetch(0, 0, cut, tile - cut, ring).start()
    for load in loads[3:]:
        load.start()
    for j in range(1, ring):
        if j == last:
            fetch(j, j % ring, 0, last_rows).start()
        elif j < last:
            fetch(j, j % ring).start()
    for load in loads[:3]:
        load.wait()
    floats = hidden_ref[...].astype(jnp.float32)
    centre = jnp.mean(floats, axis=1, keepdims=True)
    spread = jnp.mean((floats - centre) ** 2, axis=1, keepdims=True)
    normed[...] = (
        (floats - centre) * (1.0 / jnp.sqrt(spread + 1e-05)) * gain_ref[...] + bias_ref[...]
    ).astype(jnp.bfloat16)
    lane = iota((tokens, LANES), 1)

    def columns(start, count):
        return pl.ds(start if isinstance(start, int) else pl.multiple_of(start, LANES), count)

    def logits_of(slot, begin, count):
        return lax.dot_general(
            normed[...], wbuf[slot, pl.ds(begin, count), :], NT,
            preferred_element_type=jnp.float32,
        )

    def split_parts(logits, start, edge):
        parts = []
        for g in range(logits.shape[1] // LANES):
            part = logits[:, g * LANES:(g + 1) * LANES]
            inside = None
            if edge and start + (g + 1) * LANES > width:
                inside = (start + g * LANES + lane) < width
            parts.append((part, inside))
        return parts

    def store(parts, start):
        shift = off[...]
        for g, (part, inside) in enumerate(parts):
            value = part - shift
            if inside is not None:
                value = jnp.where(inside, value, 0.0)
            xsend[:, columns(start + g * LANES, LANES)] = value.astype(jnp.bfloat16)

    def send(start, count, piece):
        for r in range(1, owners):
            to = peer(r)
            pltpu.make_async_remote_copy(
                src_ref=xsend.at[
                    pl.ds(pl.multiple_of(to * slab, slab), slab), columns(start, count)
                ],
                dst_ref=xrecv.at[my_rows, columns(start, count)],
                send_sem=send_sem.at[r],
                recv_sem=recv_sem.at[piece],
                device_id=(to, mine),
                device_id_type=MESH,
            ).start()
        pltpu.make_async_copy(
            xsend.at[my_rows, columns(start, count)],
            xrecv.at[my_rows, columns(start, count)],
            recv_sem.at[piece],
        ).start()

    def gather_stats(parts, start):
        old_top = tops[...]
        new_top = old_top
        kept = []
        for part, inside in parts:
            if inside is not None:
                part = jnp.where(inside, part, LOW)
            kept.append(part)
            new_top = jnp.maximum(new_top, part)
        acc = sums[...] * jnp.exp(old_top - new_top)
        hit = hits[...]
        wanted = ids[...] - (mine * width + start)
        for g, (part, inside) in enumerate(parts):
            acc = acc + jnp.exp(kept[g] - new_top)
            match = (g * LANES + lane) == wanted
            if inside is not None:
                match = match & inside
            hit = hit + jnp.where(match, part, 0.0)
        tops[...] = new_top
        sums[...] = acc
        hits[...] = hit

    fetch(0, 0, 0, cut).wait()
    logits = logits_of(0, 0, cut)
    total = logits[:, :LANES]
    for g in range(1, cut // LANES):
        total = total + logits[:, g * LANES:(g + 1) * LANES]
    off[...] = jnp.broadcast_to(
        jnp.sum(total, axis=1, keepdims=True) * (1.0 / cut), off.shape
    )
    parts = split_parts(logits, 0, False)
    store(parts, 0)
    pl.semaphore_wait(barrier, owners + shards - 2)
    send(0, cut, 0)
    for r in range(1, owners):
        pl.semaphore_signal(ready, inc=1, device_id=(peer(r), mine), device_id_type=MESH)
    for load in loads[3:]:
        load.wait()
    wide = jnp.broadcast_to(ids_ref[...].astype(jnp.float32), (LANES, tokens))
    ids[...] = jnp.transpose(wide).astype(jnp.int32)
    tops[...] = jnp.full_like(tops, LOW)
    sums[...] = jnp.zeros_like(sums)
    hits[...] = jnp.zeros_like(hits)

    fetch(0, 0, cut, tile - cut, ring).wait()
    more = logits_of(0, cut, tile - cut)
    more_parts = split_parts(more, cut, False)
    store(more_parts, cut)
    send(cut, tile - cut, 1)
    gather_stats(parts, 0)
    gather_stats(more_parts, cut)
    if ring == last:
        fetch(last, 0, 0, last_rows).start()
    elif ring < last:
        fetch(ring, 0).start()

    held = max(1, last - HOLD)

    def middle(j, carry):
        slot = lax.rem(j, ring)
        start = j * tile
        fetch(j, slot).wait()
        chunk_parts = split_parts(logits_of(slot, 0, tile), start, False)
        store(chunk_parts, start)

        @pl.when(j < held)
        def _():
            send(start, tile, j + 1)

        gather_stats(chunk_parts, start)

        @pl.when(j + ring < last)
        def _():
            fetch(j + ring, slot).start()

        @pl.when(j + ring == last)
        def _():
            fetch(last, slot, 0, last_rows).start()

        return carry

    lax.fori_loop(1, last, middle, 0)
    tail_at = last * tile
    fetch(last, last % ring, 0, last_rows).wait()
    tail_parts = split_parts(logits_of(last % ring, 0, tile), tail_at, True)
    store(tail_parts, tail_at)
    gather_stats(tail_parts, tail_at)

    top = jnp.max(tops[...], axis=1, keepdims=True)
    total = jnp.sum(sums[...] * jnp.exp(tops[...] - top), axis=1, keepdims=True)
    picked = jnp.sum(hits[...], axis=1, keepdims=True)
    stat[...] = jnp.transpose(
        jnp.where(
            lane == 0, top,
            jnp.where(lane == 1, total, jnp.where(lane == 2, picked, off[...])),
        )
    )[0:8, :]
    sent = []
    for r in range(1, shards):
        copy = pltpu.make_async_remote_copy(
            src_ref=stat,
            dst_ref=stats.at[r - 1],
            send_sem=ssend.at[r - 1],
            recv_sem=srecv.at[r - 1],
            device_id=(me, side(r)),
            device_id_type=MESH,
        )
        copy.start()
        sent.append(copy)

    to_flat[...] = (iota((rows, flats), 0) // slab == iota((rows, flats), 1) % owners).astype(
        jnp.bfloat16
    )
    from_flat[...] = (
        iota((flats, rows), 0) % owners == iota((flats, rows), 1) // slab
    ).astype(jnp.bfloat16)
    at_steps = spread_steps(steps_ref, (kinds, LANES))
    cosines = jnp.cos(
        jnp.pi * (iota((kinds, LANES), 0) + 1).astype(jnp.float32) * at_steps / 143000.0
    )
    level = jnp.sum(
        jnp.where(iota((kinds, LANES), 1) < owners, cosines, 0.0), axis=1, keepdims=True
    ) * (1.0 / owners)
    for d in range(owners):
        basis[d] = jnp.broadcast_to(cosines[:, d:d + 1] - level, (kinds, rows))

    for copy in sent:
        copy.wait()
    best = stat[0:1, :]
    for r in range(shards - 1):
        best = jnp.maximum(best, stats[r][0:1, :])
    total = stat[1:2, :] * jnp.exp(stat[0:1, :] - best)
    picked = stat[2:3, :]
    for r in range(shards - 1):
        total = total + stats[r][1:2, :] * jnp.exp(stats[r][0:1, :] - best)
        picked = picked + stats[r][2:3, :]
    lse = best + jnp.log(total)
    dsend[...] = stat[3:4, :] - lse
    for r in range(1, owners):
        pltpu.make_async_remote_copy(
            src_ref=dsend,
            dst_ref=drecv.at[me],
            send_sem=dssem.at[0],
            recv_sem=drsem.at[0],
            device_id=(peer(r), mine),
            device_id_type=MESH,
        ).start()
    pltpu.make_async_copy(dsend, drecv.at[me], drsem.at[0]).start()

    def late(j, carry):
        send(j * tile, tile, j + 1)
        return carry

    lax.fori_loop(held, last, late, 0)
    send(tail_at, tile - cut, chunks)
    send(tail_at + tile - cut, cut, chunks + 1)
    target_ref[...] = picked - lse

    pltpu.make_async_copy(drecv, drecv, drsem.at[0]).wait()
    d = drecv[...]
    d = jnp.broadcast_to(d - jnp.mean(d, axis=0, keepdims=True), (owners, slab, tokens))
    here = iota(d.shape, 2) == me * slab + iota(d.shape, 1)
    d = jnp.sum(jnp.where(here, d, 0.0), axis=2, keepdims=True)
    dcol[...] = jnp.broadcast_to(d, (owners, slab, LANES)).reshape(rows, LANES)

    def absorb(start, count, piece, products, edge=False):
        block = xrecv.at[:, columns(start, count)]
        pltpu.make_async_copy(block, block, recv_sem.at[piece]).wait()
        level = dcol[...].reshape(owners, slab, LANES)
        for g in range(count // LANES):
            at = columns(start + g * LANES, LANES)
            x = xrecv[:, at].astype(jnp.float32).reshape(owners, slab, LANES)
            x = x - jnp.mean(x, axis=0, keepdims=True) + level
            if edge and start + (g + 1) * LANES > width:
                x = jnp.where(start + g * LANES + iota(x.shape, 2) < width, x, 0.0)
            xrecv[:, at] = x.reshape(rows, LANES).astype(jnp.bfloat16)
        kept = xrecv[:, columns(start, count)]
        pltpu.make_async_copy(block, xout_ref.at[:, columns(start, count)], out_sem.at[0]).start()
        return products + lax.dot_general(kept, kept, NT, preferred_element_type=jnp.float32)

    products = absorb(0, cut, 0, jnp.zeros((rows, rows), jnp.float32))
    products = absorb(cut, tile - cut, 1, products)
    products = lax.fori_loop(
        1, last, lambda j, p: absorb(j * tile, tile, j + 1, p), products
    )
    products = absorb(tail_at, tile - cut, chunks, products, True)
    products = absorb(tail_at + tile - cut, cut, chunks + 1, products, True)

    matched = iota((rows, rows), 0) % slab == iota((rows, rows), 1) % slab
    partial = jnp.sum(
        jnp.where(matched, products, 0.0).reshape(owners, slab, rows), axis=1
    )
    flat_own = iota((owners, flats), 1) // owners == iota((owners, flats), 0)
    gsend[...] = jnp.sum(
        jnp.where(flat_own, select_sum(partial, to_flat[...]), 0.0), axis=0, keepdims=True
    )
    slot = mine * owners + me
    pl.semaphore_wait(ready, owners - 1)
    for q in range(shards):
        for r in range(owners):
            @pl.when(slot != q * owners + r)
            def _(q=q, r=r):
                pltpu.make_async_remote_copy(
                    src_ref=gsend,
                    dst_ref=grecv.at[slot],
                    send_sem=gssem.at[0],
                    recv_sem=grsem.at[0],
                    device_id=(jnp.int32(r), jnp.int32(q)),
                    device_id_type=MESH,
                ).start()

    pltpu.make_async_copy(gsend, grecv.at[slot], grsem.at[0]).start()
    for r in range(1, owners):
        strip = xsend.at[my_rows, :]
        pltpu.make_async_copy(strip, strip, send_sem.at[r]).wait()
    others = pl.ds(0, owners - 1)
    pltpu.make_async_copy(drecv.at[others], drecv.at[others], dssem.at[0]).wait()
    row_k = iota((kinds, slab, rows), 0)
    keep = (iota((kinds, slab, rows), 2) % slab == iota((kinds, slab, rows), 1)) & (
        row_k < comps_ref[0]
    )
    flat_diag = iota((1, flats), 1) // owners == iota((1, flats), 1) % owners

    pltpu.make_async_copy(grecv, grecv, grsem.at[0]).wait()
    flat = jnp.sum(grecv[...], axis=0) * (1.0 / (tokens * width * shards))
    trace = jnp.sum(jnp.where(flat_diag, flat, 0.0), axis=1, keepdims=True)
    gexp = select_sum(
        jnp.where(flat_own, jnp.broadcast_to(flat, flat_own.shape), 0.0), from_flat[...]
    )
    mixed = basis[0] * gexp[0:1, :]
    for d in range(1, owners):
        mixed = mixed + basis[d] * gexp[d:d + 1, :]
    mixed = mixed * (1.0 / (trace * (1.0 / owners) + 1e-06) * (1.0 / owners))
    spreadout = jnp.where(
        keep, jnp.broadcast_to(mixed.reshape(kinds, 1, rows), keep.shape), 0.0
    ).reshape(kinds * slab, rows)
    high, low = halves(spreadout)
    w2_ref[:, 0:rows] = high
    w2_ref[:, rows:] = low
    gexp_ref[...] = gexp
    pltpu.make_async_copy(xrecv, xout_ref, out_sem.at[0]).wait()
    less = pl.ds(0, owners * shards - 1)
    pltpu.make_async_copy(grecv.at[less], grecv.at[less], gssem.at[0]).wait()


def mix_pieces(tiles):
    pieces = []
    for most in [6, 12] + [18] * tiles:
        if tiles:
            pieces.append(min(most, tiles))
            tiles -= pieces[-1]
    return pieces


def mix_kernel(
    width, x_ref, w2_ref, gexp_ref, target_in, out_ref, gram_ref, target_ref,
    held, gram, sem, small_sem,
):
    at = 0
    copies = [pltpu.make_async_copy(target_in, target_ref, small_sem.at[0])]
    copies[0].start()

    def send_gram():
        owners, rows = gexp_ref.shape
        pick = (
            lax.broadcasted_iota(jnp.int32, (rows, LANES), 0)
            == lax.broadcasted_iota(jnp.int32, (rows, LANES), 1) * (rows // owners)
        ).astype(jnp.float32)
        gram[...] = jnp.dot(
            gexp_ref[...], pick, precision=lax.Precision.HIGHEST,
            preferred_element_type=jnp.float32,
        )[:, :owners]
        copies.append(pltpu.make_async_copy(gram, gram_ref, small_sem.at[1]))
        copies[-1].start()

    pieces = mix_pieces(held.shape[1] // LANES)
    for i, tiles in enumerate(pieces):
        if i == min(3, len(pieces) - 1):
            send_gram()
        count = tiles * LANES
        x = x_ref[:, at:at + count]
        held[:, at:at + count] = jnp.dot(
            w2_ref[...], jnp.concatenate([x, x], axis=0), preferred_element_type=jnp.float32
        ).astype(jnp.bfloat16)
        span = pl.ds(at, count)
        if at + count > width:
            span = pl.ds(at, pl.multiple_of(count + pl.program_id(0) * LANES, LANES))
        copy = pltpu.make_async_copy(held.at[:, span], out_ref.at[:, span], sem.at[i])
        copy.start()
        copies.append(copy)
        at += count
    for copy in copies:
        copy.wait()


def per_device(owners, shards, hidden_rows, norm_gain, norm_bias, unembed, target_ids, ckpt_steps, components):
    tokens, depth = hidden_rows.shape[1:]
    width = unembed.shape[2]
    slab = tokens // owners
    rows = owners * slab
    out_rows = COMPONENTS * slab
    tile, chunks = split_tiles(width)
    padded = tile * chunks
    flats = max(owners * owners, LANES)
    ring = min(RING, chunks)
    sizes = (owners, shards, tokens, width, tile, chunks)
    f32, bf16 = jnp.float32, jnp.bfloat16
    vmem = pl.BlockSpec(memory_space=pltpu.VMEM)
    hbm = pl.BlockSpec(memory_space=pltpu.HBM)
    dma = pltpu.SemaphoreType.DMA
    limit = 67043328 - min(depth * width * 2 - (1 << 20), 16 << 20)

    def far(a):
        return pltpu.with_memory_space_constraint(a, pltpu.HBM)

    x, w2, gexp, target = pl.pallas_call(
        functools.partial(gather_kernel, sizes),
        in_specs=[hbm] * 5 + [pl.BlockSpec(memory_space=pltpu.SMEM), hbm],
        out_specs=[pl.BlockSpec(memory_space=pl.ANY), vmem, vmem, vmem],
        out_shape=[
            jax.ShapeDtypeStruct((rows, padded), bf16),
            jax.ShapeDtypeStruct((out_rows, 2 * rows), bf16),
            jax.ShapeDtypeStruct((owners, rows), f32),
            jax.ShapeDtypeStruct((1, tokens), f32),
        ],
        scratch_shapes=[
            pltpu.VMEM((tokens, depth), bf16),
            pltpu.VMEM((ring, tile, depth), bf16),
            pltpu.VMEM((tokens, padded), bf16),
            pltpu.VMEM((rows, padded), bf16),
            pltpu.VMEM((tokens, LANES), f32),
            pltpu.VMEM((tokens, LANES), jnp.int32),
            pltpu.VMEM((tokens, LANES), f32),
            pltpu.VMEM((tokens, LANES), f32),
            pltpu.VMEM((tokens, LANES), f32),
            pltpu.VMEM((8, tokens), f32),
            pltpu.VMEM((shards - 1, 8, tokens), f32),
            pltpu.VMEM((1, tokens), f32),
            pltpu.VMEM((owners, 1, tokens), f32),
            pltpu.VMEM((rows, LANES), f32),
            pltpu.VMEM((1, flats), f32),
            pltpu.VMEM((owners * shards, 1, flats), f32),
            pltpu.VMEM((owners, COMPONENTS, rows), f32),
            pltpu.VMEM((rows, flats), bf16),
            pltpu.VMEM((flats, rows), bf16),
            pltpu.VMEM((tokens, depth), bf16),
            pltpu.VMEM((1, depth), f32),
            pltpu.VMEM((1, depth), f32),
            pltpu.VMEM((1, tokens), jnp.int32),
            pltpu.SMEM((owners,), jnp.int32),
            dma((5,)), dma((ring + 1,)),
            dma((owners,)), dma((chunks + 2,)),
            dma((shards - 1,)), dma((shards - 1,)),
            dma((1,)), dma((1,)), dma((1,)), dma((1,)), dma((1,)),
            pltpu.SemaphoreType.REGULAR,
        ],
        compiler_params=pltpu.CompilerParams(
            collective_id=0, has_side_effects=True, vmem_limit_bytes=limit,
        ),
    )(
        far(hidden_rows[0]), far(norm_gain), far(norm_bias),
        far(target_ids.reshape(1, tokens)), far(ckpt_steps), components, far(unembed[0].T),
    )

    out, gram, target = pl.pallas_call(
        functools.partial(mix_kernel, width),
        grid=(1,),
        in_specs=[vmem] * 4,
        out_specs=[hbm, hbm, hbm],
        out_shape=[
            jax.ShapeDtypeStruct((out_rows, width), bf16),
            jax.ShapeDtypeStruct((owners, owners), f32),
            jax.ShapeDtypeStruct((1, tokens), f32),
        ],
        scratch_shapes=[
            pltpu.VMEM((out_rows, padded), bf16),
            pltpu.VMEM((owners, owners), f32),
            dma((len(mix_pieces(padded // LANES)),)), dma((2,)),
        ],
        compiler_params=pltpu.CompilerParams(
            dimension_semantics=("arbitrary",),
            vmem_limit_bytes=2 * (rows + out_rows) * padded + (16 << 20),
        ),
    )(x, w2, gexp, target)
    return out.reshape(COMPONENTS, slab, width), gram, target


def solution(mesh):
    return jax.shard_map(
        functools.partial(per_device, mesh.shape["ckpt"], mesh.shape["vocab"]),
        mesh=mesh,
        in_specs=(
            P("ckpt", None, None),
            P("ckpt", None),
            P("ckpt", None),
            P("ckpt", None, "vocab"),
            P(),
            P(),
            P(),
        ),
        out_specs=(P(None, "ckpt", "vocab"), P(), P("ckpt", None)),
        check_vma=False,
    )
```

```python
import functools

import jax
import jax.numpy as jnp
from jax import lax
from jax.experimental import pallas as pl
from jax.experimental.pallas import tpu as pltpu
from jax.sharding import PartitionSpec as P

COMPONENTS = 8
LANES = 128
MESH = pl.DeviceIdType.MESH
LOW = -1e30
NT = (((1,), (1,)), ((), ()))
RING = 4
HOLD = 2
DETOUR = 2
DETOUR_TILES = 3


def split_tiles(width):
    tiles = -(-width // LANES)
    best = tiles
    for per in range(1, tiles + 1):
        if tiles % per == 0 and per >= 6:
            best = per
            break
    return best * LANES, tiles // best


def spread_steps(steps_ref, shape):
    lane_owner = lax.broadcasted_iota(jnp.int32, shape, 1) % steps_ref.shape[0]
    out = jnp.zeros(shape, jnp.float32)
    for c in range(steps_ref.shape[0]):
        out = jnp.where(lane_owner == c, steps_ref[c].astype(jnp.float32), out)
    return out


def halves(value):
    high = value.astype(jnp.bfloat16)
    return high, (value - high.astype(jnp.float32)).astype(jnp.bfloat16)


def select_sum(value, table):
    count = value.shape[0]
    both = jnp.dot(
        jnp.concatenate(halves(value), axis=0), table, preferred_element_type=jnp.float32
    )
    return both[:count] + both[count:]


def gather_kernel(
    sizes,
    hidden_hbm, gain_hbm, bias_hbm, ids_hbm, steps_hbm, comps_ref, w_hbm,
    xout_ref, w2_ref, gexp_ref, target_ref,
    normed, wbuf, xsend, xrecv, off, ids, tops, sums, hits, stat, stats, dsend, drecv, dcol, relay,
    gsend, grecv, basis, to_flat, from_flat,
    hidden_ref, gain_ref, bias_ref, ids_ref, steps_ref, in_sem, wsem,
    send_sem, recv_sem, ssend, srecv, dssem, drsem, gssem, grsem, out_sem, ready, rssem, rrsem, fsem,
):
    owners, shards, tokens, width, tile, chunks = sizes
    slab = tokens // owners
    rows = owners * slab
    kinds = COMPONENTS
    ring = wbuf.shape[0]
    cut = (tile // LANES // 3) * LANES
    flats = gsend.shape[1]
    me = lax.axis_index("ckpt")
    mine = lax.axis_index("vocab")
    my_rows = pl.ds(pl.multiple_of(me * slab, slab), slab)
    last = chunks - 1
    last_rows = width - last * tile

    def peer(r):
        return lax.rem(me + r, owners)

    def side(r):
        return lax.rem(mine + r, shards)

    detour = relay.shape[1]
    held = max(1, last - HOLD)
    detouring = shards > 1 and held > DETOUR
    first_shard = (mine == 0) & detouring
    last_shard = (mine == shards - 1) & detouring

    def iota(shape, axis):
        return lax.broadcasted_iota(jnp.int32, shape, axis)

    def fetch(j, slot, begin=0, count=None, sem=None):
        count = tile if count is None else count
        start = j * tile + begin
        return pltpu.make_async_copy(
            w_hbm.at[pl.ds(start if isinstance(start, int) else pl.multiple_of(start, LANES), count), :],
            wbuf.at[slot, pl.ds(begin, count), :],
            wsem.at[slot if sem is None else sem],
        )

    loads = []
    for i, (src, dst) in enumerate((
        (hidden_hbm, hidden_ref), (gain_hbm, gain_ref), (bias_hbm, bias_ref),
        (ids_hbm, ids_ref), (steps_hbm, steps_ref),
    )):
        loads.append(pltpu.make_async_copy(src, dst, in_sem.at[i]))
    for load in loads[:3]:
        load.start()
    fetch(0, 0, 0, cut).start()
    barrier = pltpu.get_barrier_semaphore()
    greeted = [(0, q) for q in range(1, shards)] + [(r, 0) for r in range(1, owners)]
    for r, q in greeted:
        pl.semaphore_signal(
            barrier, inc=1, device_id=(peer(r), side(q)), device_id_type=MESH
        )
    fetch(0, 0, cut, tile - cut, ring).start()
    for load in loads[3:]:
        load.start()
    for j in range(1, ring):
        if j == last:
            fetch(j, j % ring, 0, last_rows).start()
        elif j < last:
            fetch(j, j % ring).start()
    for load in loads[:3]:
        load.wait()
    floats = hidden_ref[...].astype(jnp.float32)
    centre = jnp.mean(floats, axis=1, keepdims=True)
    spread = jnp.mean((floats - centre) ** 2, axis=1, keepdims=True)
    normed[...] = (
        (floats - centre) * (1.0 / jnp.sqrt(spread + 1e-05)) * gain_ref[...] + bias_ref[...]
    ).astype(jnp.bfloat16)
    lane = iota((tokens, LANES), 1)

    def columns(start, count):
        return pl.ds(start if isinstance(start, int) else pl.multiple_of(start, LANES), count)

    def logits_of(slot, begin, count):
        return lax.dot_general(
            normed[...], wbuf[slot, pl.ds(begin, count), :], NT,
            preferred_element_type=jnp.float32,
        )

    def split_parts(logits, start, edge):
        parts = []
        for g in range(logits.shape[1] // LANES):
            part = logits[:, g * LANES:(g + 1) * LANES]
            inside = None
            if edge and start + (g + 1) * LANES > width:
                inside = (start + g * LANES + lane) < width
            parts.append((part, inside))
        return parts

    def store(parts, start):
        shift = off[...]
        for g, (part, inside) in enumerate(parts):
            value = part - shift
            if inside is not None:
                value = jnp.where(inside, value, 0.0)
            xsend[:, columns(start + g * LANES, LANES)] = value.astype(jnp.bfloat16)

    def keep_own(start, count, piece):
        pltpu.make_async_copy(
            xsend.at[my_rows, columns(start, count)],
            xrecv.at[my_rows, columns(start, count)],
            recv_sem.at[piece],
        ).start()

    def send(start, count, piece):
        for r in range(1, owners):
            to = peer(r)
            pltpu.make_async_remote_copy(
                src_ref=xsend.at[
                    pl.ds(pl.multiple_of(to * slab, slab), slab), columns(start, count)
                ],
                dst_ref=xrecv.at[my_rows, columns(start, count)],
                send_sem=send_sem.at[r],
                recv_sem=recv_sem.at[piece],
                device_id=(to, mine),
                device_id_type=MESH,
            ).start()
        keep_own(start, count, piece)

    def forward():
        start = DETOUR * tile
        several = relay.at[pl.ds(0, rows - slab), :]
        pltpu.make_async_copy(several, several, rrsem.at[0]).wait()
        for r in range(1, owners):
            strip = pl.ds(pl.multiple_of(peer(r) * slab, slab), slab)
            pltpu.make_async_remote_copy(
                src_ref=relay.at[strip, :],
                dst_ref=xrecv.at[strip, columns(start, detour)],
                send_sem=fsem.at[0],
                recv_sem=recv_sem.at[DETOUR + 1],
                device_id=(me, jnp.int32(shards - 1)),
                device_id_type=MESH,
            ).start()

    def gather_stats(parts, start):
        old_top = tops[...]
        new_top = old_top
        kept = []
        for part, inside in parts:
            if inside is not None:
                part = jnp.where(inside, part, LOW)
            kept.append(part)
            new_top = jnp.maximum(new_top, part)
        acc = sums[...] * jnp.exp(old_top - new_top)
        hit = hits[...]
        wanted = ids[...] - (mine * width + start)
        for g, (part, inside) in enumerate(parts):
            acc = acc + jnp.exp(kept[g] - new_top)
            match = (g * LANES + lane) == wanted
            if inside is not None:
                match = match & inside
            hit = hit + jnp.where(match, part, 0.0)
        tops[...] = new_top
        sums[...] = acc
        hits[...] = hit

    fetch(0, 0, 0, cut).wait()
    logits = logits_of(0, 0, cut)
    total = logits[:, :LANES]
    for g in range(1, cut // LANES):
        total = total + logits[:, g * LANES:(g + 1) * LANES]
    off[...] = jnp.broadcast_to(
        jnp.sum(total, axis=1, keepdims=True) * (1.0 / cut), off.shape
    )
    parts = split_parts(logits, 0, False)
    store(parts, 0)
    pl.semaphore_wait(barrier, owners + shards - 2)
    send(0, cut, 0)
    for r in range(1, owners):
        pl.semaphore_signal(ready, inc=1, device_id=(peer(r), mine), device_id_type=MESH)
    fetch(0, 0, cut, tile - cut, ring).wait()
    more = logits_of(0, cut, tile - cut)
    more_parts = split_parts(more, cut, False)
    store(more_parts, cut)
    send(cut, tile - cut, 1)
    for load in loads[3:]:
        load.wait()
    wide = jnp.broadcast_to(ids_ref[...].astype(jnp.float32), (LANES, tokens))
    ids[...] = jnp.transpose(wide).astype(jnp.int32)
    tops[...] = jnp.full_like(tops, LOW)
    sums[...] = jnp.zeros_like(sums)
    hits[...] = jnp.zeros_like(hits)
    gather_stats(parts, 0)
    gather_stats(more_parts, cut)
    if ring == last:
        fetch(last, 0, 0, last_rows).start()
    elif ring < last:
        fetch(ring, 0).start()

    pl.semaphore_wait(ready, owners - 1)

    def middle(j, carry):
        slot = lax.rem(j, ring)
        start = j * tile
        fetch(j, slot).wait()
        chunk_parts = split_parts(logits_of(slot, 0, tile), start, False)
        store(chunk_parts, start)

        @pl.when((j < held) & jnp.logical_not(last_shard & (j == DETOUR)))
        def _():
            send(start, tile, j + 1)

        @pl.when(last_shard & (j == DETOUR))
        def _():
            keep_own(start, detour, j + 1)
            for r in range(1, owners):
                to = peer(r)
                pltpu.make_async_remote_copy(
                    src_ref=xsend.at[
                        pl.ds(pl.multiple_of(to * slab, slab), slab), columns(start, detour)
                    ],
                    dst_ref=relay.at[my_rows, :],
                    send_sem=rssem.at[0],
                    recv_sem=rrsem.at[0],
                    device_id=(to, jnp.int32(0)),
                    device_id_type=MESH,
                ).start()
            send(start + detour, tile - detour, j + 1)

        gather_stats(chunk_parts, start)

        @pl.when(j + ring < last)
        def _():
            fetch(j + ring, slot).start()

        @pl.when(j + ring == last)
        def _():
            fetch(last, slot, 0, last_rows).start()

        return carry

    lax.fori_loop(1, last, middle, 0)
    tail_at = last * tile
    fetch(last, last % ring, 0, last_rows).wait()
    tail_parts = split_parts(logits_of(last % ring, 0, tile), tail_at, True)
    store(tail_parts, tail_at)
    gather_stats(tail_parts, tail_at)

    top = jnp.max(tops[...], axis=1, keepdims=True)
    total = jnp.sum(sums[...] * jnp.exp(tops[...] - top), axis=1, keepdims=True)
    picked = jnp.sum(hits[...], axis=1, keepdims=True)
    stat[...] = jnp.transpose(
        jnp.where(
            lane == 0, top,
            jnp.where(lane == 1, total, jnp.where(lane == 2, picked, off[...])),
        )
    )[0:8, :]
    sent = []
    for r in range(1, shards):
        copy = pltpu.make_async_remote_copy(
            src_ref=stat,
            dst_ref=stats.at[r - 1],
            send_sem=ssend.at[r - 1],
            recv_sem=srecv.at[r - 1],
            device_id=(me, side(r)),
            device_id_type=MESH,
        )
        copy.start()
        sent.append(copy)

    to_flat[...] = (iota((rows, flats), 0) // slab == iota((rows, flats), 1) % owners).astype(
        jnp.bfloat16
    )
    from_flat[...] = (
        iota((flats, rows), 0) % owners == iota((flats, rows), 1) // slab
    ).astype(jnp.bfloat16)
    at_steps = spread_steps(steps_ref, (kinds, LANES))
    cosines = jnp.cos(
        jnp.pi * (iota((kinds, LANES), 0) + 1).astype(jnp.float32) * at_steps / 143000.0
    )
    level = jnp.sum(
        jnp.where(iota((kinds, LANES), 1) < owners, cosines, 0.0), axis=1, keepdims=True
    ) * (1.0 / owners)
    for d in range(owners):
        basis[d] = jnp.broadcast_to(cosines[:, d:d + 1] - level, (kinds, rows))

    for copy in sent:
        copy.wait()
    best = stat[0:1, :]
    for r in range(shards - 1):
        best = jnp.maximum(best, stats[r][0:1, :])
    total = stat[1:2, :] * jnp.exp(stat[0:1, :] - best)
    picked = stat[2:3, :]
    for r in range(shards - 1):
        total = total + stats[r][1:2, :] * jnp.exp(stats[r][0:1, :] - best)
        picked = picked + stats[r][2:3, :]
    lse = best + jnp.log(total)
    dsend[...] = stat[3:4, :] - lse
    for r in range(1, owners):
        pltpu.make_async_remote_copy(
            src_ref=dsend,
            dst_ref=drecv.at[me],
            send_sem=dssem.at[0],
            recv_sem=drsem.at[0],
            device_id=(peer(r), mine),
            device_id_type=MESH,
        ).start()
    pltpu.make_async_copy(dsend, drecv.at[me], drsem.at[0]).start()

    def late(j, carry):
        send(j * tile, tile, j + 1)
        return carry

    lax.fori_loop(held, last, late, 0)
    send(tail_at, tile - cut, chunks)
    send(tail_at + tile - cut, cut, chunks + 1)
    pl.when(first_shard)(forward)
    target_ref[...] = picked - lse

    pltpu.make_async_copy(drecv, drecv, drsem.at[0]).wait()
    d = drecv[...]
    d = jnp.broadcast_to(d - jnp.mean(d, axis=0, keepdims=True), (owners, slab, tokens))
    here = iota(d.shape, 2) == me * slab + iota(d.shape, 1)
    d = jnp.sum(jnp.where(here, d, 0.0), axis=2, keepdims=True)
    dcol[...] = jnp.broadcast_to(d, (owners, slab, LANES)).reshape(rows, LANES)

    def absorb(start, count, piece, products, edge=False):
        block = xrecv.at[:, columns(start, count)]
        pltpu.make_async_copy(block, block, recv_sem.at[piece]).wait()
        level = dcol[...].reshape(owners, slab, LANES)
        for g in range(count // LANES):
            at = columns(start + g * LANES, LANES)
            x = xrecv[:, at].astype(jnp.float32).reshape(owners, slab, LANES)
            x = x - jnp.mean(x, axis=0, keepdims=True) + level
            if edge and start + (g + 1) * LANES > width:
                x = jnp.where(start + g * LANES + iota(x.shape, 2) < width, x, 0.0)
            xrecv[:, at] = x.reshape(rows, LANES).astype(jnp.bfloat16)
        kept = xrecv[:, columns(start, count)]
        pltpu.make_async_copy(block, xout_ref.at[:, columns(start, count)], out_sem.at[0]).start()
        return products + lax.dot_general(kept, kept, NT, preferred_element_type=jnp.float32)

    products = absorb(0, cut, 0, jnp.zeros((rows, rows), jnp.float32))
    products = absorb(cut, tile - cut, 1, products)
    products = lax.fori_loop(
        1, last, lambda j, p: absorb(j * tile, tile, j + 1, p), products
    )
    products = absorb(tail_at, tile - cut, chunks, products, True)
    products = absorb(tail_at + tile - cut, cut, chunks + 1, products, True)

    matched = iota((rows, rows), 0) % slab == iota((rows, rows), 1) % slab
    partial = jnp.sum(
        jnp.where(matched, products, 0.0).reshape(owners, slab, rows), axis=1
    )
    flat_own = iota((owners, flats), 1) // owners == iota((owners, flats), 0)
    gsend[...] = jnp.sum(
        jnp.where(flat_own, select_sum(partial, to_flat[...]), 0.0), axis=0, keepdims=True
    )
    slot = mine * owners + me
    for q in range(shards):
        for r in range(owners):
            @pl.when(slot != q * owners + r)
            def _(q=q, r=r):
                pltpu.make_async_remote_copy(
                    src_ref=gsend,
                    dst_ref=grecv.at[slot],
                    send_sem=gssem.at[0],
                    recv_sem=grsem.at[0],
                    device_id=(jnp.int32(r), jnp.int32(q)),
                    device_id_type=MESH,
                ).start()

    pltpu.make_async_copy(gsend, grecv.at[slot], grsem.at[0]).start()
    @pl.when(last_shard)
    def _():
        several = relay.at[pl.ds(0, rows - slab), :]
        pltpu.make_async_copy(several, several, rssem.at[0]).wait()
        for r in range(1, owners):
            strip = xsend.at[my_rows, columns(0, tile * chunks - detour)]
            pltpu.make_async_copy(strip, strip, send_sem.at[r]).wait()

    @pl.when(jnp.logical_not(last_shard))
    def _():
        for r in range(1, owners):
            strip = xsend.at[my_rows, :]
            pltpu.make_async_copy(strip, strip, send_sem.at[r]).wait()

    @pl.when(first_shard)
    def _():
        sent_on = relay.at[pl.ds(0, rows - slab), :]
        pltpu.make_async_copy(sent_on, sent_on, fsem.at[0]).wait()

    others = pl.ds(0, owners - 1)
    pltpu.make_async_copy(drecv.at[others], drecv.at[others], dssem.at[0]).wait()
    row_k = iota((kinds, slab, rows), 0)
    keep = (iota((kinds, slab, rows), 2) % slab == iota((kinds, slab, rows), 1)) & (
        row_k < comps_ref[0]
    )
    flat_diag = iota((1, flats), 1) // owners == iota((1, flats), 1) % owners

    pltpu.make_async_copy(grecv, grecv, grsem.at[0]).wait()
    flat = jnp.sum(grecv[...], axis=0) * (1.0 / (tokens * width * shards))
    trace = jnp.sum(jnp.where(flat_diag, flat, 0.0), axis=1, keepdims=True)
    gexp = select_sum(
        jnp.where(flat_own, jnp.broadcast_to(flat, flat_own.shape), 0.0), from_flat[...]
    )
    mixed = basis[0] * gexp[0:1, :]
    for d in range(1, owners):
        mixed = mixed + basis[d] * gexp[d:d + 1, :]
    mixed = mixed * (1.0 / (trace * (1.0 / owners) + 1e-06) * (1.0 / owners))
    spreadout = jnp.where(
        keep, jnp.broadcast_to(mixed.reshape(kinds, 1, rows), keep.shape), 0.0
    ).reshape(kinds * slab, rows)
    high, low = halves(spreadout)
    w2_ref[:, 0:rows] = high
    w2_ref[:, rows:] = low
    gexp_ref[...] = gexp
    pltpu.make_async_copy(xrecv, xout_ref, out_sem.at[0]).wait()
    less = pl.ds(0, owners * shards - 1)
    pltpu.make_async_copy(grecv.at[less], grecv.at[less], gssem.at[0]).wait()


def mix_pieces(tiles):
    pieces = []
    for most in [6, 12] + [18] * tiles:
        if tiles:
            pieces.append(min(most, tiles))
            tiles -= pieces[-1]
    return pieces


def mix_kernel(
    width, x_ref, w2_ref, gexp_ref, target_in, out_ref, gram_ref, target_ref,
    held, gram, sem, small_sem,
):
    at = 0
    copies = [pltpu.make_async_copy(target_in, target_ref, small_sem.at[0])]
    copies[0].start()

    def send_gram():
        owners, rows = gexp_ref.shape
        pick = (
            lax.broadcasted_iota(jnp.int32, (rows, LANES), 0)
            == lax.broadcasted_iota(jnp.int32, (rows, LANES), 1) * (rows // owners)
        ).astype(jnp.float32)
        gram[...] = jnp.dot(
            gexp_ref[...], pick, precision=lax.Precision.HIGHEST,
            preferred_element_type=jnp.float32,
        )[:, :owners]
        copies.append(pltpu.make_async_copy(gram, gram_ref, small_sem.at[1]))
        copies[-1].start()

    pieces = mix_pieces(held.shape[1] // LANES)
    for i, tiles in enumerate(pieces):
        if i == min(3, len(pieces) - 1):
            send_gram()
        count = tiles * LANES
        x = x_ref[:, at:at + count]
        held[:, at:at + count] = jnp.dot(
            w2_ref[...], jnp.concatenate([x, x], axis=0), preferred_element_type=jnp.float32
        ).astype(jnp.bfloat16)
        span = pl.ds(at, count)
        if at + count > width:
            span = pl.ds(at, pl.multiple_of(count + pl.program_id(0) * LANES, LANES))
        copy = pltpu.make_async_copy(held.at[:, span], out_ref.at[:, span], sem.at[i])
        copy.start()
        copies.append(copy)
        at += count
    for copy in copies:
        copy.wait()


def per_device(owners, shards, hidden_rows, norm_gain, norm_bias, unembed, target_ids, ckpt_steps, components):
    tokens, depth = hidden_rows.shape[1:]
    width = unembed.shape[2]
    slab = tokens // owners
    rows = owners * slab
    out_rows = COMPONENTS * slab
    tile, chunks = split_tiles(width)
    padded = tile * chunks
    flats = max(owners * owners, LANES)
    ring = min(RING, chunks)
    sizes = (owners, shards, tokens, width, tile, chunks)
    f32, bf16 = jnp.float32, jnp.bfloat16
    vmem = pl.BlockSpec(memory_space=pltpu.VMEM)
    hbm = pl.BlockSpec(memory_space=pltpu.HBM)
    dma = pltpu.SemaphoreType.DMA
    limit = 67043328 - min(depth * width * 2 - (1 << 20), 16 << 20)

    def far(a):
        return pltpu.with_memory_space_constraint(a, pltpu.HBM)

    x, w2, gexp, target = pl.pallas_call(
        functools.partial(gather_kernel, sizes),
        in_specs=[hbm] * 5 + [pl.BlockSpec(memory_space=pltpu.SMEM), hbm],
        out_specs=[pl.BlockSpec(memory_space=pl.ANY), vmem, vmem, vmem],
        out_shape=[
            jax.ShapeDtypeStruct((rows, padded), bf16),
            jax.ShapeDtypeStruct((out_rows, 2 * rows), bf16),
            jax.ShapeDtypeStruct((owners, rows), f32),
            jax.ShapeDtypeStruct((1, tokens), f32),
        ],
        scratch_shapes=[
            pltpu.VMEM((tokens, depth), bf16),
            pltpu.VMEM((ring, tile, depth), bf16),
            pltpu.VMEM((tokens, padded), bf16),
            pltpu.VMEM((rows, padded), bf16),
            pltpu.VMEM((tokens, LANES), f32),
            pltpu.VMEM((tokens, LANES), jnp.int32),
            pltpu.VMEM((tokens, LANES), f32),
            pltpu.VMEM((tokens, LANES), f32),
            pltpu.VMEM((tokens, LANES), f32),
            pltpu.VMEM((8, tokens), f32),
            pltpu.VMEM((shards - 1, 8, tokens), f32),
            pltpu.VMEM((1, tokens), f32),
            pltpu.VMEM((owners, 1, tokens), f32),
            pltpu.VMEM((rows, LANES), f32),
            pltpu.VMEM((tokens, DETOUR_TILES * LANES), bf16),
            pltpu.VMEM((1, flats), f32),
            pltpu.VMEM((owners * shards, 1, flats), f32),
            pltpu.VMEM((owners, COMPONENTS, rows), f32),
            pltpu.VMEM((rows, flats), bf16),
            pltpu.VMEM((flats, rows), bf16),
            pltpu.VMEM((tokens, depth), bf16),
            pltpu.VMEM((1, depth), f32),
            pltpu.VMEM((1, depth), f32),
            pltpu.VMEM((1, tokens), jnp.int32),
            pltpu.SMEM((owners,), jnp.int32),
            dma((5,)), dma((ring + 1,)),
            dma((owners,)), dma((chunks + 2,)),
            dma((shards - 1,)), dma((shards - 1,)),
            dma((1,)), dma((1,)), dma((1,)), dma((1,)), dma((1,)),
            pltpu.SemaphoreType.REGULAR, dma((1,)), dma((1,)), dma((1,)),
        ],
        compiler_params=pltpu.CompilerParams(
            collective_id=0, has_side_effects=True, vmem_limit_bytes=limit,
        ),
    )(
        far(hidden_rows[0]), far(norm_gain), far(norm_bias),
        far(target_ids.reshape(1, tokens)), far(ckpt_steps), components, far(unembed[0].T),
    )

    out, gram, target = pl.pallas_call(
        functools.partial(mix_kernel, width),
        grid=(1,),
        in_specs=[vmem] * 4,
        out_specs=[hbm, hbm, hbm],
        out_shape=[
            jax.ShapeDtypeStruct((out_rows, width), bf16),
            jax.ShapeDtypeStruct((owners, owners), f32),
            jax.ShapeDtypeStruct((1, tokens), f32),
        ],
        scratch_shapes=[
            pltpu.VMEM((out_rows, padded), bf16),
            pltpu.VMEM((owners, owners), f32),
            dma((len(mix_pieces(padded // LANES)),)), dma((2,)),
        ],
        compiler_params=pltpu.CompilerParams(
            dimension_semantics=("arbitrary",),
            vmem_limit_bytes=2 * (rows + out_rows) * padded + (16 << 20),
        ),
    )(x, w2, gexp, target)
    return out.reshape(COMPONENTS, slab, width), gram, target


def solution(mesh):
    return jax.shard_map(
        functools.partial(per_device, mesh.shape["ckpt"], mesh.shape["vocab"]),
        mesh=mesh,
        in_specs=(
            P("ckpt", None, None),
            P("ckpt", None),
            P("ckpt", None),
            P("ckpt", None, "vocab"),
            P(),
            P(),
            P(),
        ),
        out_specs=(P(None, "ckpt", "vocab"), P(), P("ckpt", None)),
        check_vma=False,
    )
```

```python
import functools

import jax
import jax.numpy as jnp
from jax import lax
from jax.experimental import pallas as pl
from jax.experimental.pallas import tpu as pltpu
from jax.sharding import PartitionSpec as P

COMPONENTS = 8
LANES = 128
MESH = pl.DeviceIdType.MESH
LOW = -1e30
NT = (((1,), (1,)), ((), ()))
RING = 4
HOLD = 2
DETOUR = 2
DETOUR_TILES = 3


def split_tiles(width):
    tiles = -(-width // LANES)
    best = tiles
    for per in range(1, tiles + 1):
        if tiles % per == 0 and per >= 6:
            best = per
            break
    return best * LANES, tiles // best


def spread_steps(steps_ref, shape):
    lane_owner = lax.broadcasted_iota(jnp.int32, shape, 1) % steps_ref.shape[0]
    out = jnp.zeros(shape, jnp.float32)
    for c in range(steps_ref.shape[0]):
        out = jnp.where(lane_owner == c, steps_ref[c].astype(jnp.float32), out)
    return out


def halves(value):
    high = value.astype(jnp.bfloat16)
    return high, (value - high.astype(jnp.float32)).astype(jnp.bfloat16)


def select_sum(value, table):
    count = value.shape[0]
    both = jnp.dot(
        jnp.concatenate(halves(value), axis=0), table, preferred_element_type=jnp.float32
    )
    return both[:count] + both[count:]


def gather_kernel(
    sizes,
    hidden_hbm, gain_hbm, bias_hbm, ids_hbm, steps_hbm, comps_ref, w_hbm,
    xout_ref, w2_ref, gexp_ref, target_ref,
    normed, wbuf, xsend, xrecv, off, ids, tops, sums, hits, stat, stats, dsend, drecv, dcol, relay,
    gsend, grecv, basis, to_flat, from_flat,
    hidden_ref, gain_ref, bias_ref, ids_ref, steps_ref, in_sem, wsem,
    send_sem, recv_sem, ssend, srecv, dssem, drsem, gssem, grsem, out_sem, ready, rssem, rrsem, fsem,
):
    owners, shards, tokens, width, tile, chunks = sizes
    slab = tokens // owners
    rows = owners * slab
    kinds = COMPONENTS
    ring = wbuf.shape[0]
    cut = (tile // LANES // 2) * LANES
    flats = gsend.shape[1]
    me = lax.axis_index("ckpt")
    mine = lax.axis_index("vocab")
    my_rows = pl.ds(pl.multiple_of(me * slab, slab), slab)
    last = chunks - 1
    last_rows = width - last * tile

    def peer(r):
        return lax.rem(me + r, owners)

    def side(r):
        return lax.rem(mine + r, shards)

    detour = relay.shape[1]
    held = max(1, last - HOLD)
    detouring = shards > 1 and held > DETOUR
    first_shard = (mine == 0) & detouring
    last_shard = (mine == shards - 1) & detouring

    def iota(shape, axis):
        return lax.broadcasted_iota(jnp.int32, shape, axis)

    def fetch(j, slot, begin=0, count=None, sem=None):
        count = tile if count is None else count
        start = j * tile + begin
        return pltpu.make_async_copy(
            w_hbm.at[pl.ds(start if isinstance(start, int) else pl.multiple_of(start, LANES), count), :],
            wbuf.at[slot, pl.ds(begin, count), :],
            wsem.at[slot if sem is None else sem],
        )

    loads = []
    for i, (src, dst) in enumerate((
        (hidden_hbm, hidden_ref), (gain_hbm, gain_ref), (bias_hbm, bias_ref),
        (ids_hbm, ids_ref), (steps_hbm, steps_ref),
    )):
        loads.append(pltpu.make_async_copy(src, dst, in_sem.at[i]))
    for load in loads[:3]:
        load.start()
    fetch(0, 0, 0, cut).start()
    barrier = pltpu.get_barrier_semaphore()
    greeted = [(0, q) for q in range(1, shards)] + [(r, 0) for r in range(1, owners)]
    for r, q in greeted:
        pl.semaphore_signal(
            barrier, inc=1, device_id=(peer(r), side(q)), device_id_type=MESH
        )
    fetch(0, 0, cut, tile - cut, ring).start()
    for load in loads[3:]:
        load.start()
    for j in range(1, ring):
        if j == last:
            fetch(j, j % ring, 0, last_rows).start()
        elif j < last:
            fetch(j, j % ring).start()
    for load in loads[:3]:
        load.wait()
    floats = hidden_ref[...].astype(jnp.float32)
    centre = jnp.mean(floats, axis=1, keepdims=True)
    spread = jnp.mean((floats - centre) ** 2, axis=1, keepdims=True)
    normed[...] = (
        (floats - centre) * (1.0 / jnp.sqrt(spread + 1e-05)) * gain_ref[...] + bias_ref[...]
    ).astype(jnp.bfloat16)
    lane = iota((tokens, LANES), 1)

    def columns(start, count):
        return pl.ds(start if isinstance(start, int) else pl.multiple_of(start, LANES), count)

    def logits_of(slot, begin, count):
        return lax.dot_general(
            normed[...], wbuf[slot, pl.ds(begin, count), :], NT,
            preferred_element_type=jnp.float32,
        )

    def split_parts(logits, start, edge):
        parts = []
        for g in range(logits.shape[1] // LANES):
            part = logits[:, g * LANES:(g + 1) * LANES]
            inside = None
            if edge and start + (g + 1) * LANES > width:
                inside = (start + g * LANES + lane) < width
            parts.append((part, inside))
        return parts

    def store(parts, start):
        shift = off[...]
        for g, (part, inside) in enumerate(parts):
            value = part - shift
            if inside is not None:
                value = jnp.where(inside, value, 0.0)
            xsend[:, columns(start + g * LANES, LANES)] = value.astype(jnp.bfloat16)

    def keep_own(start, count, piece):
        pltpu.make_async_copy(
            xsend.at[my_rows, columns(start, count)],
            xrecv.at[my_rows, columns(start, count)],
            recv_sem.at[piece],
        ).start()

    def send(start, count, piece):
        for r in range(1, owners):
            to = peer(r)
            pltpu.make_async_remote_copy(
                src_ref=xsend.at[
                    pl.ds(pl.multiple_of(to * slab, slab), slab), columns(start, count)
                ],
                dst_ref=xrecv.at[my_rows, columns(start, count)],
                send_sem=send_sem.at[r],
                recv_sem=recv_sem.at[piece],
                device_id=(to, mine),
                device_id_type=MESH,
            ).start()
        keep_own(start, count, piece)

    def forward():
        start = DETOUR * tile
        several = relay.at[pl.ds(0, rows - slab), :]
        pltpu.make_async_copy(several, several, rrsem.at[0]).wait()
        for r in range(1, owners):
            strip = pl.ds(pl.multiple_of(peer(r) * slab, slab), slab)
            pltpu.make_async_remote_copy(
                src_ref=relay.at[strip, :],
                dst_ref=xrecv.at[strip, columns(start, detour)],
                send_sem=fsem.at[0],
                recv_sem=recv_sem.at[DETOUR + 1],
                device_id=(me, jnp.int32(shards - 1)),
                device_id_type=MESH,
            ).start()

    def gather_stats(parts, start):
        old_top = tops[...]
        new_top = old_top
        kept = []
        for part, inside in parts:
            if inside is not None:
                part = jnp.where(inside, part, LOW)
            kept.append(part)
            new_top = jnp.maximum(new_top, part)
        acc = sums[...] * jnp.exp(old_top - new_top)
        hit = hits[...]
        wanted = ids[...] - (mine * width + start)
        for g, (part, inside) in enumerate(parts):
            acc = acc + jnp.exp(kept[g] - new_top)
            match = (g * LANES + lane) == wanted
            if inside is not None:
                match = match & inside
            hit = hit + jnp.where(match, part, 0.0)
        tops[...] = new_top
        sums[...] = acc
        hits[...] = hit

    fetch(0, 0, 0, cut).wait()
    logits = logits_of(0, 0, cut)
    total = logits[:, :LANES]
    for g in range(1, cut // LANES):
        total = total + logits[:, g * LANES:(g + 1) * LANES]
    off[...] = jnp.broadcast_to(
        jnp.sum(total, axis=1, keepdims=True) * (1.0 / cut), off.shape
    )
    parts = split_parts(logits, 0, False)
    store(parts, 0)
    pl.semaphore_wait(barrier, owners + shards - 2)
    send(0, cut, 0)
    for r in range(1, owners):
        pl.semaphore_signal(ready, inc=1, device_id=(peer(r), mine), device_id_type=MESH)
    fetch(0, 0, cut, tile - cut, ring).wait()
    more = logits_of(0, cut, tile - cut)
    more_parts = split_parts(more, cut, False)
    store(more_parts, cut)
    send(cut, tile - cut, 1)
    for load in loads[3:]:
        load.wait()
    wide = jnp.broadcast_to(ids_ref[...].astype(jnp.float32), (LANES, tokens))
    ids[...] = jnp.transpose(wide).astype(jnp.int32)
    tops[...] = jnp.full_like(tops, LOW)
    sums[...] = jnp.zeros_like(sums)
    hits[...] = jnp.zeros_like(hits)
    gather_stats(parts, 0)
    gather_stats(more_parts, cut)
    if ring == last:
        fetch(last, 0, 0, last_rows).start()
    elif ring < last:
        fetch(ring, 0).start()

    pl.semaphore_wait(ready, owners - 1)

    def middle(j, carry):
        slot = lax.rem(j, ring)
        start = j * tile
        fetch(j, slot).wait()
        chunk_parts = split_parts(logits_of(slot, 0, tile), start, False)
        store(chunk_parts, start)

        @pl.when((j < held) & jnp.logical_not(last_shard & (j == DETOUR)))
        def _():
            send(start, tile, j + 1)

        @pl.when(last_shard & (j == DETOUR))
        def _():
            keep_own(start, detour, j + 1)
            for r in range(1, owners):
                to = peer(r)
                pltpu.make_async_remote_copy(
                    src_ref=xsend.at[
                        pl.ds(pl.multiple_of(to * slab, slab), slab), columns(start, detour)
                    ],
                    dst_ref=relay.at[my_rows, :],
                    send_sem=rssem.at[0],
                    recv_sem=rrsem.at[0],
                    device_id=(to, jnp.int32(0)),
                    device_id_type=MESH,
                ).start()
            send(start + detour, tile - detour, j + 1)

        gather_stats(chunk_parts, start)

        @pl.when(j + ring < last)
        def _():
            fetch(j + ring, slot).start()

        @pl.when(j + ring == last)
        def _():
            fetch(last, slot, 0, last_rows).start()

        return carry

    lax.fori_loop(1, last, middle, 0)
    tail_at = last * tile
    fetch(last, last % ring, 0, last_rows).wait()
    tail_parts = split_parts(logits_of(last % ring, 0, tile), tail_at, True)
    store(tail_parts, tail_at)
    gather_stats(tail_parts, tail_at)

    top = jnp.max(tops[...], axis=1, keepdims=True)
    total = jnp.sum(sums[...] * jnp.exp(tops[...] - top), axis=1, keepdims=True)
    picked = jnp.sum(hits[...], axis=1, keepdims=True)
    stat[...] = jnp.transpose(
        jnp.where(
            lane == 0, top,
            jnp.where(lane == 1, total, jnp.where(lane == 2, picked, off[...])),
        )
    )[0:8, :]
    sent = []
    for r in range(1, shards):
        copy = pltpu.make_async_remote_copy(
            src_ref=stat,
            dst_ref=stats.at[r - 1],
            send_sem=ssend.at[r - 1],
            recv_sem=srecv.at[r - 1],
            device_id=(me, side(r)),
            device_id_type=MESH,
        )
        copy.start()
        sent.append(copy)

    to_flat[...] = (iota((rows, flats), 0) // slab == iota((rows, flats), 1) % owners).astype(
        jnp.bfloat16
    )
    from_flat[...] = (
        iota((flats, rows), 0) % owners == iota((flats, rows), 1) // slab
    ).astype(jnp.bfloat16)
    at_steps = spread_steps(steps_ref, (kinds, LANES))
    cosines = jnp.cos(
        jnp.pi * (iota((kinds, LANES), 0) + 1).astype(jnp.float32) * at_steps / 143000.0
    )
    level = jnp.sum(
        jnp.where(iota((kinds, LANES), 1) < owners, cosines, 0.0), axis=1, keepdims=True
    ) * (1.0 / owners)
    for d in range(owners):
        basis[d] = jnp.broadcast_to(cosines[:, d:d + 1] - level, (kinds, rows))

    for copy in sent:
        copy.wait()
    best = stat[0:1, :]
    for r in range(shards - 1):
        best = jnp.maximum(best, stats[r][0:1, :])
    total = stat[1:2, :] * jnp.exp(stat[0:1, :] - best)
    picked = stat[2:3, :]
    for r in range(shards - 1):
        total = total + stats[r][1:2, :] * jnp.exp(stats[r][0:1, :] - best)
        picked = picked + stats[r][2:3, :]
    lse = best + jnp.log(total)
    dsend[...] = stat[3:4, :] - lse
    for r in range(1, owners):
        pltpu.make_async_remote_copy(
            src_ref=dsend,
            dst_ref=drecv.at[me],
            send_sem=dssem.at[0],
            recv_sem=drsem.at[0],
            device_id=(peer(r), mine),
            device_id_type=MESH,
        ).start()
    pltpu.make_async_copy(dsend, drecv.at[me], drsem.at[0]).start()

    def late(j, carry):
        send(j * tile, tile, j + 1)
        return carry

    lax.fori_loop(held, last, late, 0)
    send(tail_at, tile - cut, chunks)
    send(tail_at + tile - cut, cut, chunks + 1)
    pl.when(first_shard)(forward)
    target_ref[...] = picked - lse

    pltpu.make_async_copy(drecv, drecv, drsem.at[0]).wait()
    d = drecv[...]
    d = jnp.broadcast_to(d - jnp.mean(d, axis=0, keepdims=True), (owners, slab, tokens))
    here = iota(d.shape, 2) == me * slab + iota(d.shape, 1)
    d = jnp.sum(jnp.where(here, d, 0.0), axis=2, keepdims=True)
    dcol[...] = jnp.broadcast_to(d, (owners, slab, LANES)).reshape(rows, LANES)

    def absorb(start, count, piece, products, edge=False):
        block = xrecv.at[:, columns(start, count)]
        pltpu.make_async_copy(block, block, recv_sem.at[piece]).wait()
        level = dcol[...].reshape(owners, slab, LANES)
        for g in range(count // LANES):
            at = columns(start + g * LANES, LANES)
            x = xrecv[:, at].astype(jnp.float32).reshape(owners, slab, LANES)
            x = x - jnp.mean(x, axis=0, keepdims=True) + level
            if edge and start + (g + 1) * LANES > width:
                x = jnp.where(start + g * LANES + iota(x.shape, 2) < width, x, 0.0)
            xrecv[:, at] = x.reshape(rows, LANES).astype(jnp.bfloat16)
        kept = xrecv[:, columns(start, count)]
        pltpu.make_async_copy(block, xout_ref.at[:, columns(start, count)], out_sem.at[0]).start()
        return products + lax.dot_general(kept, kept, NT, preferred_element_type=jnp.float32)

    products = absorb(0, cut, 0, jnp.zeros((rows, rows), jnp.float32))
    products = absorb(cut, tile - cut, 1, products)
    products = lax.fori_loop(
        1, last, lambda j, p: absorb(j * tile, tile, j + 1, p), products
    )
    products = absorb(tail_at, tile - cut, chunks, products, True)
    products = absorb(tail_at + tile - cut, cut, chunks + 1, products, True)

    matched = iota((rows, rows), 0) % slab == iota((rows, rows), 1) % slab
    partial = jnp.sum(
        jnp.where(matched, products, 0.0).reshape(owners, slab, rows), axis=1
    )
    flat_own = iota((owners, flats), 1) // owners == iota((owners, flats), 0)
    gsend[...] = jnp.sum(
        jnp.where(flat_own, select_sum(partial, to_flat[...]), 0.0), axis=0, keepdims=True
    )
    slot = mine * owners + me
    for q in range(shards):
        for r in range(owners):
            @pl.when(slot != q * owners + r)
            def _(q=q, r=r):
                pltpu.make_async_remote_copy(
                    src_ref=gsend,
                    dst_ref=grecv.at[slot],
                    send_sem=gssem.at[0],
                    recv_sem=grsem.at[0],
                    device_id=(jnp.int32(r), jnp.int32(q)),
                    device_id_type=MESH,
                ).start()

    pltpu.make_async_copy(gsend, grecv.at[slot], grsem.at[0]).start()
    @pl.when(last_shard)
    def _():
        several = relay.at[pl.ds(0, rows - slab), :]
        pltpu.make_async_copy(several, several, rssem.at[0]).wait()
        for r in range(1, owners):
            strip = xsend.at[my_rows, columns(0, tile * chunks - detour)]
            pltpu.make_async_copy(strip, strip, send_sem.at[r]).wait()

    @pl.when(jnp.logical_not(last_shard))
    def _():
        for r in range(1, owners):
            strip = xsend.at[my_rows, :]
            pltpu.make_async_copy(strip, strip, send_sem.at[r]).wait()

    @pl.when(first_shard)
    def _():
        sent_on = relay.at[pl.ds(0, rows - slab), :]
        pltpu.make_async_copy(sent_on, sent_on, fsem.at[0]).wait()

    others = pl.ds(0, owners - 1)
    pltpu.make_async_copy(drecv.at[others], drecv.at[others], dssem.at[0]).wait()
    row_k = iota((kinds, slab, rows), 0)
    keep = (iota((kinds, slab, rows), 2) % slab == iota((kinds, slab, rows), 1)) & (
        row_k < comps_ref[0]
    )
    flat_diag = iota((1, flats), 1) // owners == iota((1, flats), 1) % owners

    pltpu.make_async_copy(grecv, grecv, grsem.at[0]).wait()
    flat = jnp.sum(grecv[...], axis=0) * (1.0 / (tokens * width * shards))
    trace = jnp.sum(jnp.where(flat_diag, flat, 0.0), axis=1, keepdims=True)
    gexp = select_sum(
        jnp.where(flat_own, jnp.broadcast_to(flat, flat_own.shape), 0.0), from_flat[...]
    )
    mixed = basis[0] * gexp[0:1, :]
    for d in range(1, owners):
        mixed = mixed + basis[d] * gexp[d:d + 1, :]
    mixed = mixed * (1.0 / (trace * (1.0 / owners) + 1e-06) * (1.0 / owners))
    spreadout = jnp.where(
        keep, jnp.broadcast_to(mixed.reshape(kinds, 1, rows), keep.shape), 0.0
    ).reshape(kinds * slab, rows)
    high, low = halves(spreadout)
    w2_ref[:, 0:rows] = high
    w2_ref[:, rows:] = low
    gexp_ref[...] = gexp
    pltpu.make_async_copy(xrecv, xout_ref, out_sem.at[0]).wait()
    less = pl.ds(0, owners * shards - 1)
    pltpu.make_async_copy(grecv.at[less], grecv.at[less], gssem.at[0]).wait()


def mix_pieces(tiles):
    pieces = []
    for most in [6, 12] + [18] * tiles:
        if tiles:
            pieces.append(min(most, tiles))
            tiles -= pieces[-1]
    return pieces


def mix_kernel(
    width, x_ref, w2_ref, gexp_ref, target_in, out_ref, gram_ref, target_ref,
    held, gram, sem, small_sem,
):
    at = 0
    copies = [pltpu.make_async_copy(target_in, target_ref, small_sem.at[0])]
    copies[0].start()

    def send_gram():
        owners, rows = gexp_ref.shape
        pick = (
            lax.broadcasted_iota(jnp.int32, (rows, LANES), 0)
            == lax.broadcasted_iota(jnp.int32, (rows, LANES), 1) * (rows // owners)
        ).astype(jnp.float32)
        gram[...] = jnp.dot(
            gexp_ref[...], pick, precision=lax.Precision.HIGHEST,
            preferred_element_type=jnp.float32,
        )[:, :owners]
        copies.append(pltpu.make_async_copy(gram, gram_ref, small_sem.at[1]))
        copies[-1].start()

    pieces = mix_pieces(held.shape[1] // LANES)
    for i, tiles in enumerate(pieces):
        if i == min(3, len(pieces) - 1):
            send_gram()
        count = tiles * LANES
        x = x_ref[:, at:at + count]
        held[:, at:at + count] = jnp.dot(
            w2_ref[...], jnp.concatenate([x, x], axis=0), preferred_element_type=jnp.float32
        ).astype(jnp.bfloat16)
        span = pl.ds(at, count)
        if at + count > width:
            span = pl.ds(at, pl.multiple_of(count + pl.program_id(0) * LANES, LANES))
        copy = pltpu.make_async_copy(held.at[:, span], out_ref.at[:, span], sem.at[i])
        copy.start()
        copies.append(copy)
        at += count
    for copy in copies:
        copy.wait()


def per_device(owners, shards, hidden_rows, norm_gain, norm_bias, unembed, target_ids, ckpt_steps, components):
    tokens, depth = hidden_rows.shape[1:]
    width = unembed.shape[2]
    slab = tokens // owners
    rows = owners * slab
    out_rows = COMPONENTS * slab
    tile, chunks = split_tiles(width)
    padded = tile * chunks
    flats = max(owners * owners, LANES)
    ring = min(RING, chunks)
    sizes = (owners, shards, tokens, width, tile, chunks)
    f32, bf16 = jnp.float32, jnp.bfloat16
    vmem = pl.BlockSpec(memory_space=pltpu.VMEM)
    hbm = pl.BlockSpec(memory_space=pltpu.HBM)
    dma = pltpu.SemaphoreType.DMA
    limit = 67043328 - min(depth * width * 2 - (1 << 20), 16 << 20)

    def far(a):
        return pltpu.with_memory_space_constraint(a, pltpu.HBM)

    x, w2, gexp, target = pl.pallas_call(
        functools.partial(gather_kernel, sizes),
        in_specs=[hbm] * 5 + [pl.BlockSpec(memory_space=pltpu.SMEM), hbm],
        out_specs=[pl.BlockSpec(memory_space=pl.ANY), vmem, vmem, vmem],
        out_shape=[
            jax.ShapeDtypeStruct((rows, padded), bf16),
            jax.ShapeDtypeStruct((out_rows, 2 * rows), bf16),
            jax.ShapeDtypeStruct((owners, rows), f32),
            jax.ShapeDtypeStruct((1, tokens), f32),
        ],
        scratch_shapes=[
            pltpu.VMEM((tokens, depth), bf16),
            pltpu.VMEM((ring, tile, depth), bf16),
            pltpu.VMEM((tokens, padded), bf16),
            pltpu.VMEM((rows, padded), bf16),
            pltpu.VMEM((tokens, LANES), f32),
            pltpu.VMEM((tokens, LANES), jnp.int32),
            pltpu.VMEM((tokens, LANES), f32),
            pltpu.VMEM((tokens, LANES), f32),
            pltpu.VMEM((tokens, LANES), f32),
            pltpu.VMEM((8, tokens), f32),
            pltpu.VMEM((shards - 1, 8, tokens), f32),
            pltpu.VMEM((1, tokens), f32),
            pltpu.VMEM((owners, 1, tokens), f32),
            pltpu.VMEM((rows, LANES), f32),
            pltpu.VMEM((tokens, DETOUR_TILES * LANES), bf16),
            pltpu.VMEM((1, flats), f32),
            pltpu.VMEM((owners * shards, 1, flats), f32),
            pltpu.VMEM((owners, COMPONENTS, rows), f32),
            pltpu.VMEM((rows, flats), bf16),
            pltpu.VMEM((flats, rows), bf16),
            pltpu.VMEM((tokens, depth), bf16),
            pltpu.VMEM((1, depth), f32),
            pltpu.VMEM((1, depth), f32),
            pltpu.VMEM((1, tokens), jnp.int32),
            pltpu.SMEM((owners,), jnp.int32),
            dma((5,)), dma((ring + 1,)),
            dma((owners,)), dma((chunks + 2,)),
            dma((shards - 1,)), dma((shards - 1,)),
            dma((1,)), dma((1,)), dma((1,)), dma((1,)), dma((1,)),
            pltpu.SemaphoreType.REGULAR, dma((1,)), dma((1,)), dma((1,)),
        ],
        compiler_params=pltpu.CompilerParams(
            collective_id=0, has_side_effects=True, vmem_limit_bytes=limit,
        ),
    )(
        far(hidden_rows[0]), far(norm_gain), far(norm_bias),
        far(target_ids.reshape(1, tokens)), far(ckpt_steps), components, far(unembed[0].T),
    )

    out, gram, target = pl.pallas_call(
        functools.partial(mix_kernel, width),
        grid=(1,),
        in_specs=[vmem] * 4,
        out_specs=[hbm, hbm, hbm],
        out_shape=[
            jax.ShapeDtypeStruct((out_rows, width), bf16),
            jax.ShapeDtypeStruct((owners, owners), f32),
            jax.ShapeDtypeStruct((1, tokens), f32),
        ],
        scratch_shapes=[
            pltpu.VMEM((out_rows, padded), bf16),
            pltpu.VMEM((owners, owners), f32),
            dma((len(mix_pieces(padded // LANES)),)), dma((2,)),
        ],
        compiler_params=pltpu.CompilerParams(
            dimension_semantics=("arbitrary",),
            vmem_limit_bytes=2 * (rows + out_rows) * padded + (16 << 20),
        ),
    )(x, w2, gexp, target)
    return out.reshape(COMPONENTS, slab, width), gram, target


def solution(mesh):
    return jax.shard_map(
        functools.partial(per_device, mesh.shape["ckpt"], mesh.shape["vocab"]),
        mesh=mesh,
        in_specs=(
            P("ckpt", None, None),
            P("ckpt", None),
            P("ckpt", None),
            P("ckpt", None, "vocab"),
            P(),
            P(),
            P(),
        ),
        out_specs=(P(None, "ckpt", "vocab"), P(), P("ckpt", None)),
        check_vma=False,
    )
```
